256 devices in a mesh: echo: 8 (over x, y_lo), coil: 16 (over z, core), read: 2 (over y_hi).
Axes of the slice: x: 4, y: 4 (y_hi: 2, y_lo: 2; y = y_hi * 2 + y_lo), z: 8, core: 2. Of those that a mesh axis runs over, the one named last changes fastest.
Arguments:
- kspace: bfloat16 [384, 8, 16, 4, 2, 192], P(None, 'echo', 'coil', 'read'), may hold values from -3 to 3
- sampling: int32 [384, 8, 192], P(None, 'echo'), may hold values 0 or 1
- coil_maps: bfloat16 [384, 16, 4, 2, 192], P(None, 'coil', 'read'), may hold values from -1.5 to 1.5
- image: float32 [384, 8, 4, 2, 192], P('coil', 'echo', 'read'), may hold values from -6 to 6
- filters: bfloat16 [48, 3, 3, 3, 2], replicated, may hold values from -0.875 to 0.875
- thresholds: float32 [48], replicated, may hold values from 0.5 to 8
- dc_weight: float32 [8], P('echo'), may hold values from 0.5 to 2
Outputs:
- updated: float32 [384, 8, 4, 2, 192], P('coil', 'echo', 'read')
The draws below stay inside these ranges and needn't reach their ends.
All inputs are finite; a program needn't handle non-finite values. No bound on the sum of `sampling` on one device may be relied on, other than what follows from the above.
Results may differ from the reference program's by a relative error of at most 0.0033.
Values may be sent and summed in bfloat16 or wider, within the bound.
No kernel may reach another device: no remote copies, remote signals or barrier semaphores. Data moves between devices by JAX's collectives and lax.ppermute only.
A program may use at most 128 MiB of HBM per device.

```python
import math
import jax
import jax.numpy as jnp
from jax import lax

NY = 384
NZ = 192
FILTERS = 48
ECHOES = 8
COILS = 16
RO = 4


def plant(values, rng, low, high):
    extent = values.shape
    index_at = [jax.random.randint(jax.random.fold_in(rng, axis), (), 0, extent[axis]) for axis in range(len(extent))]
    values = values.at[tuple(index_at)].set(low)
    longest = extent.index(max(extent))
    index_at[longest] = (index_at[longest] + 1) % extent[longest]
    return values.at[tuple(index_at)].set(high)


def shard_levels(rng, dims, shards, smallest, largest):
    def one(axis_at, shards_of):
        steps = jax.random.uniform(jax.random.fold_in(jax.random.fold_in(rng, 6), axis_at), (shards_of,), jnp.float32, smallest / len(shards), largest / len(shards))
        return jnp.repeat(jnp.exp(steps), dims[axis_at] // shards_of).reshape((-1,) + (1,) * (len(dims) - axis_at - 1))

    factor_of = one(*shards[0])
    for cut in shards[1:]:
        factor_of = factor_of * one(*cut)
    return factor_of


def noise(key, dims, scale, reach, cuts=(), held_as=jnp.bfloat16):
    drawn = scale * jax.random.normal(key, dims, jnp.float32)
    if cuts:
        drawn = drawn * shard_levels(key, dims, cuts, -0.22, 0.18)
    return jnp.clip(drawn, -reach, reach).astype(held_as)


def setup_inputs(seed: int = 0) -> dict:
    keys = jax.random.split(jax.random.key(seed), 8)
    kspace = noise(keys[0], (NY, ECHOES, COILS, RO, 2, NZ), 0.5, 3.0, ((1, 8), (2, 16), (3, 2)))
    sampling = plant((jax.random.randint(keys[1], (NY, ECHOES, NZ), 0, 3) < 1).astype(jnp.int32), jax.random.fold_in(keys[1], 1), 0, 1)
    coil_maps = noise(keys[2], (NY, COILS, RO, 2, NZ), 0.25, 1.5, ((1, 16), (2, 2)))
    image = noise(keys[3], (NY, ECHOES, RO, 2, NZ), 1.0, 6.0, ((0, 16), (1, 8), (2, 2)), jnp.float32)
    filters = noise(keys[4], (FILTERS, 3, 3, 3, 2), 54 ** -0.5, 0.875)
    thresholds = jnp.clip(jnp.exp(jax.random.uniform(keys[5], (FILTERS,), jnp.float32, math.log(0.5), math.log(8.0))), 0.5, 8.0)
    dc_weight = jnp.clip(jnp.exp(math.log(2.0) - 1.3862944 * jax.random.uniform(keys[6], (ECHOES,), jnp.float32) ** shard_levels(keys[6], (ECHOES,), ((0, 8),), -0.2, 0.2)), 0.5, 2.0)
    return {"kspace": kspace, "sampling": sampling, "coil_maps": coil_maps, "image": image, "filters": filters, "thresholds": thresholds, "dc_weight": dc_weight}


def tables(length):
    positions = jnp.arange(length, dtype=jnp.int32)
    product = positions[:, None] * positions[None, :] % length
    phases = product.astype(jnp.float32) * (2.0 * jnp.pi / length)
    normalize = length ** (-0.5)
    return (jnp.cos(phases) * normalize, jnp.sin(phases) * normalize)

def complex_times(left, right, conjugate):
    left_real = left[..., 0, :]
    left_imag = left[..., 1, :]
    right_real = right[..., 0, :]
    right_imag = right[..., 1, :]
    if conjugate:
        return jnp.stack([left_real * right_real + left_imag * right_imag, left_real * right_imag - left_imag * right_real], -2)
    return jnp.stack([left_real * right_real - left_imag * right_imag, left_real * right_imag + left_imag * right_real], -2)

def column_section(values, block):
    shape = values.shape
    merged = values.reshape(shape[:-2] + (shape[-2] * shape[-1],)).astype(jnp.float32)
    result = jnp.dot(merged, block.astype(jnp.float32))
    return result.reshape(shape)

def row_section(values, row_table, adjoint):
    lines = values.shape[0]
    result = jnp.einsum('ay,y...->a...', row_table.astype(jnp.float32), values.astype(jnp.float32))
    cosine_part = result[:lines]
    sine_part = result[lines:]
    if adjoint:
        return jnp.stack([cosine_part[..., 0, :] - sine_part[..., 1, :], cosine_part[..., 1, :] + sine_part[..., 0, :]], -2)
    return jnp.stack([cosine_part[..., 0, :] + sine_part[..., 1, :], cosine_part[..., 1, :] - sine_part[..., 0, :]], -2)

def reference(kspace, sampling, coil_maps, image, filters, thresholds, dc_weight):
    row_cos, row_sin = tables(NY)
    row_table = jnp.concatenate([row_cos, row_sin], 0).astype(jnp.bfloat16)
    col_cos, col_sin = tables(NZ)
    forward_block = jnp.block([[col_cos, -col_sin], [col_sin, col_cos]]).astype(jnp.bfloat16)
    adjoint_block = jnp.block([[col_cos, col_sin], [-col_sin, col_cos]]).astype(jnp.bfloat16)
    rounded = image.astype(jnp.bfloat16)
    sampled = sampling.astype(jnp.float32)[:, :, None, None, :]

    def per_coil(summed, coil_index):
        sensitivity = lax.dynamic_index_in_dim(coil_maps, coil_index, 1, keepdims=False).astype(jnp.float32)
        measured = lax.dynamic_index_in_dim(kspace, coil_index, 2, keepdims=False).astype(jnp.float32)
        weighted = complex_times(sensitivity[:, None], rounded.astype(jnp.float32), False).astype(jnp.bfloat16)
        halfway = column_section(weighted, forward_block).astype(jnp.bfloat16)
        spectrum = row_section(halfway, row_table, False)
        residual = (sampled * (spectrum - measured)).astype(jnp.bfloat16)
        backward = row_section(residual, row_table, True).astype(jnp.bfloat16)
        restored = column_section(backward, adjoint_block)
        return (summed + complex_times(sensitivity[:, None], restored, True), None)
    adjoint, _ = lax.scan(per_coil, jnp.zeros(image.shape, jnp.float32), jnp.arange(COILS, dtype=jnp.int32))
    padded = jnp.pad(rounded, ((1, 1), (0, 0), (1, 1), (0, 0), (1, 1))).astype(jnp.float32)
    lines, echoes, slices, parts, columns = image.shape

    def per_filter(summed, filter_pair):
        kernel, threshold = filter_pair
        kernel = kernel.astype(jnp.float32)
        response = jnp.zeros((lines, echoes, slices, columns), jnp.float32)
        for shift_y in range(3):
            for shift_r in range(3):
                for shift_z in range(3):
                    window = padded[shift_y:shift_y + lines, :, shift_r:shift_r + slices, :, shift_z:shift_z + columns]
                    response = response + kernel[shift_y, shift_r, shift_z, 0] * window[:, :, :, 0] + kernel[shift_y, shift_r, shift_z, 1] * window[:, :, :, 1]
        magnitude = jnp.sqrt(lax.optimization_barrier(jnp.sum(response * response, axis=1)))
        factor = magnitude / (magnitude + threshold)
        shrunk = (response * factor[:, None]).astype(jnp.bfloat16).astype(jnp.float32)
        shrunk_pad = jnp.pad(shrunk, ((1, 1), (0, 0), (1, 1), (1, 1)))
        contribution = jnp.zeros(image.shape, jnp.float32)
        for shift_y in range(3):
            for shift_r in range(3):
                for shift_z in range(3):
                    window = shrunk_pad[2 - shift_y:2 - shift_y + lines, :, 2 - shift_r:2 - shift_r + slices, 2 - shift_z:2 - shift_z + columns]
                    contribution = contribution + jnp.stack([kernel[shift_y, shift_r, shift_z, 0] * window, kernel[shift_y, shift_r, shift_z, 1] * window], -2)
        return (summed + contribution, None)
    penalty, _ = lax.scan(per_filter, jnp.zeros(image.shape, jnp.float32), (filters, thresholds))
    return image - dc_weight[None, :, None, None, None] * adjoint - penalty
```

```python
import functools

import jax
import jax.numpy as jnp
import ml_dtypes
import numpy as np
from jax import lax
from jax.experimental import pallas as pl
from jax.experimental.pallas import tpu as pltpu
from jax.sharding import PartitionSpec as P

NY = 384
NZ = 192
FILTERS = 48
ECHOES = 8
COILS = 16
ROWS = NY // COILS
HALO = 2
BAND = 8
WINDOW = BAND + 2
SITES = 3 * FILTERS
BASES = (0, 8, 16, 18)
FIRST = (0, 0, 0, 6)

bf16 = jnp.bfloat16
f32 = jnp.float32


def np_tables(length):
    positions = np.arange(length, dtype=np.int32)
    product = positions[:, None] * positions[None, :] % length
    phases = product.astype(np.float32) * np.float32(2.0 * np.pi / length)
    normalize = np.float32(length ** (-0.5))
    cos = (np.cos(phases) * normalize).astype(ml_dtypes.bfloat16)
    sin = (np.sin(phases) * normalize).astype(ml_dtypes.bfloat16)
    return cos, sin


def np_expansions():
    respond = np.zeros((2, BAND * 3, 54, 256), np.float32)
    spread = np.zeros((2, BAND * 3, 54, 128), np.float32)
    for read in range(2):
        for t in range(BAND):
            for site in range(3):
                for a in range(3):
                    for b in range(3):
                        for d in range(3):
                            for p in range(2):
                                tap = ((a * 3 + b) * 3 + d) * 2 + p
                                sigma = read + site + b - 1
                                if 0 <= sigma < 4:
                                    column = ((d * 2 + sigma // 2) * WINDOW + t + a) * 4
                                    column += (sigma % 2) * 2 + p
                                    respond[read, t * 3 + site, tap, column] = 1
                                own = b + site - read - 1
                                if 0 <= own < 2:
                                    row = (d * WINDOW + t + a) * 4 + own * 2 + p
                                    spread[read, t * 3 + site, tap, row] = 1
    return respond.astype(ml_dtypes.bfloat16), spread.astype(ml_dtypes.bfloat16)


def consistency_kernel(x_ref, mine_ref, other_ref, sampling_ref, row_ref, col_ref, out_ref):
    def dot(left, right):
        return jnp.dot(left, right, preferred_element_type=f32)

    x_real = x_ref[:, 0].astype(f32).reshape(NY, NZ)
    x_imag = x_ref[:, 1].astype(f32).reshape(NY, NZ)
    sampled = sampling_ref[...].astype(f32)
    row = row_ref[...]
    col_cos = col_ref[0]
    col_sin = col_ref[1]
    sum_real = jnp.zeros((NY, NZ), f32)
    sum_imag = jnp.zeros((NY, NZ), f32)
    for ref in (mine_ref, other_ref):
        map_real = ref[2].astype(f32)
        map_imag = ref[3].astype(f32)
        w_real = (map_real * x_real - map_imag * x_imag).astype(bf16)
        w_imag = (map_real * x_imag + map_imag * x_real).astype(bf16)
        h_real = (dot(w_real, col_cos) + dot(w_imag, col_sin)).astype(bf16)
        h_imag = (dot(w_imag, col_cos) - dot(w_real, col_sin)).astype(bf16)
        s_real = dot(row, jnp.concatenate([h_real, h_imag], 0))
        s_imag = dot(row, jnp.concatenate([h_imag, -h_real], 0))
        r_real = (sampled * (s_real - ref[0].astype(f32))).astype(bf16)
        r_imag = (sampled * (s_imag - ref[1].astype(f32))).astype(bf16)
        b_real = dot(row, jnp.concatenate([r_real, -r_imag], 0)).astype(bf16)
        b_imag = dot(row, jnp.concatenate([r_imag, r_real], 0)).astype(bf16)
        o_real = dot(b_real, col_cos) - dot(b_imag, col_sin)
        o_imag = dot(b_real, col_sin) + dot(b_imag, col_cos)
        sum_real = sum_real + map_real * o_real + map_imag * o_imag
        sum_imag = sum_imag + map_real * o_imag - map_imag * o_real
    out_ref[:, 0] = sum_real.reshape(COILS, ROWS, NZ).astype(bf16)
    out_ref[:, 1] = sum_imag.reshape(COILS, ROWS, NZ).astype(bf16)


def consistency(x, mine, other, sampling, row, col):
    return pl.pallas_call(
        consistency_kernel,
        out_shape=jax.ShapeDtypeStruct((COILS, 2, ROWS, NZ), bf16),
        in_specs=[pl.BlockSpec(memory_space=pltpu.VMEM)] * 6,
        out_specs=pl.BlockSpec(memory_space=pltpu.VMEM),
        compiler_params=pltpu.CompilerParams(vmem_limit_bytes=40 << 20),
        cost_estimate=pl.CostEstimate(
            flops=4_000_000_000, bytes_accessed=3_000_000, transcendentals=0
        ),
        name="consistency",
    )(x, mine, other, sampling, row, col)


def regularizer_kernel(
    place_ref, x_ref, weights_ref, spread_ref, thresholds_ref, out_ref, shifted_ref, total_ref
):
    me = place_ref[0]
    for e in range(ECHOES):
        x = x_ref[e].astype(f32)
        zero = jnp.zeros((2, 28 * 4, 1), f32)
        shifted_ref[e, 0] = jnp.concatenate([zero, x[:, :, : NZ - 1]], 2).astype(bf16)
        shifted_ref[e, 1] = x_ref[e]
        shifted_ref[e, 2] = jnp.concatenate([x[:, :, 1:], zero], 2).astype(bf16)
    total_ref[...] = jnp.zeros_like(total_ref)

    def windows(e, base):
        block = shifted_ref[e, :, :, base * 4 : (base + WINDOW) * 4, :]
        return block.reshape(3 * 2 * WINDOW * 4, NZ)

    for base, first in zip(BASES, FIRST):
        weights = weights_ref[first * SITES :, : 3 * 2 * WINDOW * 4]
        energy = None
        for e in range(ECHOES):
            response = jnp.dot(weights, windows(e, base), preferred_element_type=f32)
            square = response * response
            energy = square if energy is None else energy + square
        response = jnp.dot(weights, windows(me, base), preferred_element_type=f32)
        magnitude = jnp.sqrt(energy)
        factor = magnitude / (magnitude + thresholds_ref[first * SITES :, :])
        shrunk = response * factor
        if base == 0:
            top = shrunk[:SITES] * place_ref[1].astype(f32)
            shrunk = jnp.concatenate([top, shrunk[SITES:]], 0)
        if base == BASES[-1]:
            bottom = shrunk[-SITES:] * place_ref[2].astype(f32)
            shrunk = jnp.concatenate([shrunk[:-SITES], bottom], 0)
        part = jnp.dot(
            spread_ref[:, first * SITES :], shrunk.astype(bf16), preferred_element_type=f32
        )
        for d in range(3):
            rows = slice(base * 4, (base + WINDOW) * 4)
            total_ref[d, rows, :] += part[d * WINDOW * 4 : (d + 1) * WINDOW * 4]
    inner = slice(HALO * 4, (HALO + ROWS) * 4)
    zero = jnp.zeros((ROWS * 4, 1), f32)
    out_ref[...] = (
        total_ref[1, inner, :]
        + jnp.concatenate([total_ref[0, inner, 1:], zero], 1)
        + jnp.concatenate([zero, total_ref[2, inner, : NZ - 1]], 1)
    )


def regularizer(place, x, weights, spread, thresholds):
    vmem = pl.BlockSpec(memory_space=pltpu.VMEM)
    return pl.pallas_call(
        regularizer_kernel,
        out_shape=jax.ShapeDtypeStruct((ROWS * 4, NZ), f32),
        in_specs=[pl.BlockSpec(memory_space=pltpu.SMEM), vmem, vmem, vmem, vmem],
        out_specs=vmem,
        scratch_shapes=[
            pltpu.VMEM((ECHOES, 3, 2, 28 * 4, NZ), bf16),
            pltpu.VMEM((3, 28 * 4, NZ), f32),
        ],
        compiler_params=pltpu.CompilerParams(vmem_limit_bytes=40 << 20),
        cost_estimate=pl.CostEstimate(
            flops=9_000_000_000, bytes_accessed=2_000_000, transcendentals=1_000_000
        ),
        name="regularizer",
    )(place, x, weights, spread, thresholds)


def body(kspace, sampling, coil_maps, image, filters, thresholds, dc_weight):
    row_cos, row_sin = np_tables(NY)
    row = jnp.asarray(np.concatenate([row_cos, row_sin], 1))
    col = jnp.asarray(np.stack(np_tables(NZ)))
    coil = lax.axis_index("coil")
    core = lax.rem(coil, 2)
    echo = lax.axis_index("echo")
    read = lax.axis_index("read")

    lines = image.reshape(ROWS * 4, NZ)
    rounded = lines.astype(bf16)
    planes = rounded.reshape(ROWS, 2, 2, NZ).transpose(1, 2, 0, 3)
    sent = jnp.broadcast_to(planes[None], (COILS // 2, 2, 2, ROWS, NZ))
    gathered = lax.all_to_all(sent.reshape(COILS, 2, ROWS, NZ), "coil", 0, 0, tiled=True)

    first = rounded[: HALO * 4]
    last = rounded[-HALO * 4 :]
    even = core == 0
    on_chip = [(i, i ^ 1) for i in range(COILS)]
    next_chip = [(i, i + 1) for i in range(1, COILS - 1, 2)]
    next_chip += [(j, i) for i, j in next_chip]
    near = lax.ppermute(jnp.where(even, last, first), "coil", on_chip)
    far = lax.ppermute(jnp.where(even, first, last), "coil", next_chip)
    above = jnp.where(even, far, near)
    below = jnp.where(even, near, far)
    extended = jnp.concatenate([above, rounded, below], 0)
    echoes = lax.all_to_all(
        jnp.broadcast_to(extended[None], (2 * ECHOES, *extended.shape)),
        ("echo", "read"),
        0,
        0,
        tiled=True,
    ).reshape(ECHOES, 2, 28 * 4, NZ)

    both = jnp.concatenate(
        [kspace[:, 0, 0].transpose(1, 2, 0, 3), coil_maps[:, 0].transpose(1, 2, 0, 3)], 1
    )
    mine = lax.dynamic_index_in_dim(both, core, 0, keepdims=False)
    other = lax.ppermute(
        lax.dynamic_index_in_dim(both, 1 - core, 0, keepdims=False), "coil", on_chip
    )
    partial = consistency(gathered, mine, other, sampling[:, 0], row, col)
    arrived = lax.all_to_all(partial, "coil", 0, 0, tiled=True)

    respond, spread = np_expansions()
    taps = filters.reshape(FILTERS, 54)
    respond = lax.dynamic_index_in_dim(jnp.asarray(respond), read, 0, keepdims=False)
    spread = lax.dynamic_index_in_dim(jnp.asarray(spread), read, 0, keepdims=False)
    weights = jnp.einsum("kc,ycl->ykl", taps, respond, preferred_element_type=f32)
    weights = weights.astype(bf16).reshape(BAND * SITES, 256)
    spread = jnp.einsum("ycl,kc->lyk", spread, taps, preferred_element_type=f32)
    spread = spread.astype(bf16).reshape(128, BAND * SITES)
    levels = jnp.broadcast_to(
        jnp.tile(thresholds, BAND * 3)[:, None], (BAND * SITES, NZ)
    )
    place = jnp.stack([echo, (coil > 0).astype(jnp.int32), (coil < COILS - 1).astype(jnp.int32)])
    penalty = regularizer(place.astype(jnp.int32), echoes, weights, spread, levels)

    summed = jnp.sum(arrived.reshape(COILS // 2, 2, 2, ROWS, NZ).astype(f32), axis=0)
    adjoint = summed.transpose(2, 0, 1, 3).reshape(ROWS * 4, NZ)
    updated = lines - dc_weight[0] * adjoint - penalty
    return updated.reshape(image.shape)


def solution(mesh):
    return jax.shard_map(
        body,
        mesh=mesh,
        in_specs=(
            P(None, "echo", "coil", "read", None, None),
            P(None, "echo", None),
            P(None, "coil", "read", None, None),
            P("coil", "echo", "read", None, None),
            P(),
            P(),
            P("echo"),
        ),
        out_specs=P("coil", "echo", "read", None, None),
        check_vma=False,
    )
```

```python
import functools

import jax
import jax.numpy as jnp
import ml_dtypes
import numpy as np
from jax import lax
from jax.experimental import pallas as pl
from jax.experimental.pallas import tpu as pltpu
from jax.sharding import PartitionSpec as P

NY = 384
NZ = 192
FILTERS = 48
ECHOES = 8
COILS = 16
ROWS = NY // COILS
HALO = 2
BAND = 8
WINDOW = BAND + 2
SITES = 3 * FILTERS
PAIR = 2
LINES = ROWS + 2 * HALO
BASES = (0, 8, 16, 18)
FIRST = (0, 0, 0, 6)

bf16 = jnp.bfloat16
f32 = jnp.float32


def np_tables(length):
    positions = np.arange(length, dtype=np.int32)
    product = positions[:, None] * positions[None, :] % length
    phases = product.astype(np.float32) * np.float32(2.0 * np.pi / length)
    normalize = np.float32(length ** (-0.5))
    cos = (np.cos(phases) * normalize).astype(ml_dtypes.bfloat16)
    sin = (np.sin(phases) * normalize).astype(ml_dtypes.bfloat16)
    return cos, sin


def np_expansions():
    respond = np.zeros((2, 3, 54, 256), np.float32)
    spread = np.zeros((2, PAIR * 3, 54, 48), np.float32)
    for read in range(2):
        for site in range(3):
            for a in range(3):
                for b in range(3):
                    for d in range(3):
                        for p in range(2):
                            tap = ((a * 3 + b) * 3 + d) * 2 + p
                            sigma = read + site + b - 1
                            if 0 <= sigma < 4:
                                half = (sigma // 2) ^ read
                                column = ((d * 2 + half) * WINDOW + a) * 4
                                column += (sigma % 2) * 2 + p
                                respond[read, site, tap, column] = 1
                            own = b + site - read - 1
                            if 0 <= own < 2:
                                for t in range(PAIR):
                                    row = (d * (PAIR + 2) + t + a) * 4 + own * 2 + p
                                    spread[read, t * 3 + site, tap, row] = 1
    return respond.astype(ml_dtypes.bfloat16), spread.astype(ml_dtypes.bfloat16)


def prepare_kernel(place_ref, image_ref, sent_ref, lines_ref, near_ref, far_ref, rows_ref):
    pad = jnp.zeros((ROWS, 256 - NZ), f32)
    for s in range(2):
        for p in range(2):
            plane = image_ref[:, 0, s, p, :]
            rows = pl.ds(s * 2 + p, ROWS, stride=4)
            rows_ref[0, rows, :] = plane[:, :128]
            rows_ref[1, rows, :] = jnp.concatenate([plane[:, 128:], pad], 1)
            plane = plane.astype(bf16)
            for z in range(COILS // 2):
                sent_ref[2 * z + s, p] = plane
    lines = jnp.concatenate([rows_ref[0], rows_ref[1, :, : NZ - 128]], 1)
    lines_ref[...] = lines.astype(bf16)
    first = lines[: HALO * 4]
    last = lines[(ROWS - HALO) * 4 :]
    even = place_ref[0] == 0
    near_ref[...] = jnp.where(even, last, first).astype(bf16)
    far_ref[...] = jnp.where(even, first, last).astype(bf16)


def prepare(place, image):
    vmem = pl.BlockSpec(memory_space=pltpu.VMEM)
    return pl.pallas_call(
        prepare_kernel,
        out_shape=(
            jax.ShapeDtypeStruct((COILS, 2, ROWS, NZ), bf16),
            jax.ShapeDtypeStruct((ROWS * 4, NZ), bf16),
            jax.ShapeDtypeStruct((HALO * 4, NZ), bf16),
            jax.ShapeDtypeStruct((HALO * 4, NZ), bf16),
        ),
        in_specs=[pl.BlockSpec(memory_space=pltpu.SMEM), vmem],
        out_specs=(vmem, vmem, vmem, vmem),
        scratch_shapes=[pltpu.VMEM((2, ROWS * 4, 128), f32)],
        compiler_params=pltpu.CompilerParams(vmem_limit_bytes=8 << 20),
        name="prepare",
    )(place, image)


def consistency_kernel(
    x_ref, sampling_ref, mine, other_hbm, row_hbm, col_hbm, out_ref, other, row_v, col_v, sem
):
    copies = [
        pltpu.make_async_copy(source, target, sem.at[i])
        for i, (source, target) in enumerate(
            ((col_hbm, col_v), (row_hbm, row_v), (other_hbm, other))
        )
    ]
    for copy in copies:
        copy.start()

    def dot(left, right):
        return jnp.dot(left, right, preferred_element_type=f32)

    x_real = x_ref[:, 0].astype(f32).reshape(NY, NZ)
    x_imag = x_ref[:, 1].astype(f32).reshape(NY, NZ)
    sampled = sampling_ref[...].astype(f32)
    sum_real = jnp.zeros((NY, NZ), f32)
    sum_imag = jnp.zeros((NY, NZ), f32)
    copies[0].wait()
    for ref in (mine, other):
        if ref is other:
            copies[2].wait()
        map_real = ref[2].astype(f32)
        map_imag = ref[3].astype(f32)
        w_real = (map_real * x_real - map_imag * x_imag).astype(bf16)
        w_imag = (map_real * x_imag + map_imag * x_real).astype(bf16)
        h_real = (dot(w_real, col_v[0]) + dot(w_imag, col_v[1])).astype(bf16)
        h_imag = (dot(w_imag, col_v[0]) - dot(w_real, col_v[1])).astype(bf16)
        if ref is mine:
            copies[1].wait()
        row = row_v[...]
        s_real = dot(row, jnp.concatenate([h_real, h_imag], 0))
        s_imag = dot(row, jnp.concatenate([h_imag, -h_real], 0))
        r_real = (sampled * (s_real - ref[0].astype(f32))).astype(bf16)
        r_imag = (sampled * (s_imag - ref[1].astype(f32))).astype(bf16)
        b_real = dot(row, jnp.concatenate([r_real, -r_imag], 0)).astype(bf16)
        b_imag = dot(row, jnp.concatenate([r_imag, r_real], 0)).astype(bf16)
        o_real = dot(b_real, col_v[0]) - dot(b_imag, col_v[1])
        o_imag = dot(b_real, col_v[1]) + dot(b_imag, col_v[0])
        sum_real = sum_real + map_real * o_real + map_imag * o_imag
        sum_imag = sum_imag + map_real * o_imag - map_imag * o_real
    out_ref[:, 0] = sum_real.reshape(COILS, ROWS, NZ).astype(bf16)
    out_ref[:, 1] = sum_imag.reshape(COILS, ROWS, NZ).astype(bf16)


def consistency(x, sampling, mine, other, row, col):
    vmem = pl.BlockSpec(memory_space=pltpu.VMEM)
    hbm = pl.BlockSpec(memory_space=pltpu.HBM)
    return pl.pallas_call(
        consistency_kernel,
        out_shape=jax.ShapeDtypeStruct((COILS, 2, ROWS, NZ), bf16),
        in_specs=[vmem, vmem, vmem, hbm, hbm, hbm],
        out_specs=vmem,
        scratch_shapes=[
            pltpu.VMEM((4, NY, NZ), bf16),
            pltpu.VMEM((NY, 2 * NY), bf16),
            pltpu.VMEM((2, NZ, NZ), bf16),
            pltpu.SemaphoreType.DMA((3,)),
        ],
        compiler_params=pltpu.CompilerParams(vmem_limit_bytes=20 << 20),
        cost_estimate=pl.CostEstimate(
            flops=4_000_000_000, bytes_accessed=3_000_000, transcendentals=0
        ),
        name="consistency",
    )(x, sampling, mine, other, row, col)


def regularizer_kernel(
    place_ref,
    x0_ref,
    x1_ref,
    x2_ref,
    x3_ref,
    taps_ref,
    respond_ref,
    spread_ref,
    thresholds_ref,
    out_ref,
    weights_ref,
    shifted_ref,
    total_ref,
):
    for site in range(3):
        taps = jnp.dot(taps_ref[...], respond_ref[site], preferred_element_type=f32)
        for t in range(BAND):
            rolled = pltpu.roll(taps, 4 * t, 1) if t else taps
            start = (t * 3 + site) * FILTERS
            weights_ref[start : start + FILTERS, :] = rolled.astype(bf16)
    zero = jnp.zeros((2, LINES * 4, 1), f32)
    for e in range(ECHOES):
        ref = (x0_ref, x1_ref, x2_ref, x3_ref)[e // 2]
        x = ref[e % 2].astype(f32)
        shifted_ref[e, 0] = jnp.concatenate([zero, x[:, :, : NZ - 1]], 2).astype(bf16)
        shifted_ref[e, 1] = ref[e % 2]
        shifted_ref[e, 2] = jnp.concatenate([x[:, :, 1:], zero], 2).astype(bf16)
    total_ref[...] = jnp.zeros_like(total_ref)
    spread = spread_ref[...]

    for base, first in zip(BASES, FIRST):
        weights = weights_ref[first * SITES :, : 3 * 2 * WINDOW * 4]
        energy = None
        for e in reversed(range(ECHOES)):
            block = shifted_ref[e, :, :, base * 4 : (base + WINDOW) * 4, :]
            window = block.reshape(3 * 2 * WINDOW * 4, NZ)
            response = jnp.dot(weights, window, preferred_element_type=f32)
            square = response * response
            energy = square if energy is None else energy + square
        magnitude = jnp.sqrt(energy)
        factor = magnitude / (magnitude + thresholds_ref[first * SITES :, :])
        shrunk = response * factor
        if base == 0:
            top = shrunk[:SITES] * place_ref[1].astype(f32)
            shrunk = jnp.concatenate([top, shrunk[SITES:]], 0)
        if base == BASES[-1]:
            bottom = shrunk[-SITES:] * place_ref[2].astype(f32)
            shrunk = jnp.concatenate([shrunk[:-SITES], bottom], 0)
        shrunk = shrunk.astype(bf16)
        for t in range(0, BAND - first, PAIR):
            pair = shrunk[t * SITES : (t + PAIR) * SITES]
            part = jnp.dot(spread, pair, preferred_element_type=f32)
            size = (PAIR + 2) * 4
            start = (base + first + t) * 4
            for d in range(3):
                total_ref[d, start : start + size, :] += part[d * size : (d + 1) * size]
    inner = slice(HALO * 4, (HALO + ROWS) * 4)
    zero = jnp.zeros((ROWS * 4, 1), f32)
    penalty = (
        total_ref[1, inner, :]
        + jnp.concatenate([total_ref[0, inner, 1:], zero], 1)
        + jnp.concatenate([zero, total_ref[2, inner, : NZ - 1]], 1)
    )
    pad = jnp.zeros((ROWS * 4, 256 - NZ), f32)
    out_ref[0] = penalty[:, :128]
    out_ref[1] = jnp.concatenate([penalty[:, 128:], pad], 1)


def regularizer(place, blocks, taps, respond, spread, thresholds):
    vmem = pl.BlockSpec(memory_space=pltpu.VMEM)
    return pl.pallas_call(
        regularizer_kernel,
        out_shape=jax.ShapeDtypeStruct((2, ROWS * 4, 128), f32),
        in_specs=[pl.BlockSpec(memory_space=pltpu.SMEM)] + [vmem] * 8,
        out_specs=vmem,
        scratch_shapes=[
            pltpu.VMEM((BAND * SITES, 256), bf16),
            pltpu.VMEM((ECHOES, 3, 2, LINES * 4, NZ), bf16),
            pltpu.VMEM((3, LINES * 4, NZ), f32),
        ],
        compiler_params=pltpu.CompilerParams(vmem_limit_bytes=20 << 20),
        cost_estimate=pl.CostEstimate(
            flops=9_000_000_000, bytes_accessed=2_000_000, transcendentals=1_000_000
        ),
        name="regularizer",
    )(place, *blocks, taps, respond, spread, thresholds)


def update_kernel(weight_ref, image_ref, arrived_ref, penalty_ref, out_ref):
    for s in range(2):
        for p in range(2):
            total = arrived_ref[s, p].astype(f32)
            for z in range(1, COILS // 2):
                total = total + arrived_ref[2 * z + s, p].astype(f32)
            rows = pl.ds(s * 2 + p, ROWS, stride=4)
            penalty = jnp.concatenate(
                [penalty_ref[0, rows, :], penalty_ref[1, rows, :][:, : NZ - 128]], 1
            )
            out_ref[:, 0, s, p, :] = image_ref[:, 0, s, p, :] - weight_ref[0] * total - penalty


def update(weight, image, arrived, penalty):
    vmem = pl.BlockSpec(memory_space=pltpu.VMEM)
    return pl.pallas_call(
        update_kernel,
        out_shape=jax.ShapeDtypeStruct(image.shape, f32),
        in_specs=[pl.BlockSpec(memory_space=pltpu.SMEM), vmem, vmem, vmem],
        out_specs=vmem,
        compiler_params=pltpu.CompilerParams(vmem_limit_bytes=8 << 20),
        name="update",
    )(weight, image, arrived, penalty)


def body(kspace, sampling, coil_maps, image, filters, thresholds, dc_weight):
    row_cos, row_sin = np_tables(NY)
    row = jnp.asarray(np.concatenate([row_cos, row_sin], 1))
    col = jnp.asarray(np.stack(np_tables(NZ)))
    coil = lax.axis_index("coil")
    core = lax.rem(coil, 2)
    read = lax.axis_index("read")
    place = jnp.stack([core, (coil > 0).astype(jnp.int32), (coil < COILS - 1).astype(jnp.int32)])

    sent, lines, near, far = prepare(place, image)
    gathered = lax.all_to_all(sent, "coil", 0, 0, tiled=True)

    even = core == 0
    on_chip = [(i, i ^ 1) for i in range(COILS)]
    next_chip = [(i, i + 1) for i in range(1, COILS - 1, 2)]
    next_chip += [(j, i) for i, j in next_chip]
    near = lax.ppermute(near, "coil", on_chip)
    far = lax.ppermute(far, "coil", next_chip)
    above = jnp.where(even, far, near)
    below = jnp.where(even, near, far)
    extended = jnp.concatenate([above, lines, below], 0)

    def swap(block, flip):
        pairs = [(i, i ^ flip) for i in range(2 * ECHOES)]
        return lax.ppermute(block, ("echo", "read"), pairs)

    quad = jnp.stack([extended] + [swap(extended, flip) for flip in (1, 8, 9)])
    quad = quad.reshape(2, 2, LINES * 4, NZ)
    blocks = [quad] + [swap(quad, flip) for flip in (2, 4, 6)]

    both = jnp.concatenate(
        [kspace[:, 0, 0].transpose(1, 2, 0, 3), coil_maps[:, 0].transpose(1, 2, 0, 3)], 1
    )
    mine = lax.dynamic_index_in_dim(both, core, 0, keepdims=False)
    other = lax.ppermute(
        lax.dynamic_index_in_dim(both, 1 - core, 0, keepdims=False), "coil", on_chip
    )
    partial = consistency(gathered, sampling[:, 0], mine, other, row, col)
    arrived = lax.all_to_all(partial, "coil", 0, 0, tiled=True)

    respond, spread = np_expansions()
    taps = filters.reshape(FILTERS, 54)
    respond = lax.dynamic_index_in_dim(jnp.asarray(respond), read, 0, keepdims=False)
    spread = lax.dynamic_index_in_dim(jnp.asarray(spread), read, 0, keepdims=False)
    spread = jnp.einsum("ycl,kc->lyk", spread, taps, preferred_element_type=f32)
    spread = spread.astype(bf16).reshape(48, PAIR * SITES)
    levels = jnp.broadcast_to(jnp.tile(thresholds, BAND * 3)[:, None], (BAND * SITES, NZ))
    penalty = regularizer(place, blocks, taps, respond, spread, levels)
    return update(dc_weight, image, arrived, penalty)


def solution(mesh):
    return jax.shard_map(
        body,
        mesh=mesh,
        in_specs=(
            P(None, "echo", "coil", "read", None, None),
            P(None, "echo", None),
            P(None, "coil", "read", None, None),
            P("coil", "echo", "read", None, None),
            P(),
            P(),
            P("echo"),
        ),
        out_specs=P("coil", "echo", "read", None, None),
        check_vma=False,
    )
```

```python
import functools

import jax
import jax.numpy as jnp
import ml_dtypes
import numpy as np
from jax import lax
from jax.experimental import pallas as pl
from jax.experimental.pallas import tpu as pltpu
from jax.sharding import PartitionSpec as P

NY = 384
NZ = 192
FILTERS = 48
ECHOES = 8
COILS = 16
ROWS = NY // COILS
HALO = 2
BAND = 8
WINDOW = BAND + 2
SITES = 3 * FILTERS
PAIR = 2
LINES = ROWS + 2 * HALO
BASES = (0, 8, 16, 18)
FIRST = (0, 0, 0, 6)

bf16 = jnp.bfloat16
f32 = jnp.float32


def np_tables(length):
    positions = np.arange(length, dtype=np.int32)
    product = positions[:, None] * positions[None, :] % length
    phases = product.astype(np.float32) * np.float32(2.0 * np.pi / length)
    normalize = np.float32(length ** (-0.5))
    cos = (np.cos(phases) * normalize).astype(ml_dtypes.bfloat16)
    sin = (np.sin(phases) * normalize).astype(ml_dtypes.bfloat16)
    return cos, sin


def np_expansions():
    respond = np.zeros((2, 3, 54, 256), np.float32)
    spread = np.zeros((2, PAIR * 3, 54, 48), np.float32)
    for read in range(2):
        for site in range(3):
            for a in range(3):
                for b in range(3):
                    for d in range(3):
                        for p in range(2):
                            tap = ((a * 3 + b) * 3 + d) * 2 + p
                            sigma = read + site + b - 1
                            if 0 <= sigma < 4:
                                half = (sigma // 2) ^ read
                                column = ((d * 2 + half) * WINDOW + a) * 4
                                column += (sigma % 2) * 2 + p
                                respond[read, site, tap, column] = 1
                            own = b + site - read - 1
                            if 0 <= own < 2:
                                for t in range(PAIR):
                                    row = (d * (PAIR + 2) + t + a) * 4 + own * 2 + p
                                    spread[read, t * 3 + site, tap, row] = 1
    return respond.astype(ml_dtypes.bfloat16), spread.astype(ml_dtypes.bfloat16)


def prepare_kernel(place_ref, image_ref, sent_ref, lines_ref, near_ref, far_ref, rows_ref):
    pad = jnp.zeros((ROWS, 256 - NZ), f32)
    for s in range(2):
        for p in range(2):
            plane = image_ref[:, 0, s, p, :]
            rows = pl.ds(s * 2 + p, ROWS, stride=4)
            rows_ref[0, rows, :] = plane[:, :128]
            rows_ref[1, rows, :] = jnp.concatenate([plane[:, 128:], pad], 1)
            plane = plane.astype(bf16)
            for z in range(COILS // 2):
                sent_ref[2 * z + s, p] = plane
    lines = jnp.concatenate([rows_ref[0], rows_ref[1, :, : NZ - 128]], 1)
    lines_ref[...] = lines.astype(bf16)
    first = lines[: HALO * 4]
    last = lines[(ROWS - HALO) * 4 :]
    even = place_ref[0] == 0
    near_ref[...] = jnp.where(even, last, first).astype(bf16)
    far_ref[...] = jnp.where(even, first, last).astype(bf16)


def prepare(place, image):
    vmem = pl.BlockSpec(memory_space=pltpu.VMEM)
    return pl.pallas_call(
        prepare_kernel,
        out_shape=(
            jax.ShapeDtypeStruct((COILS, 2, ROWS, NZ), bf16),
            jax.ShapeDtypeStruct((ROWS * 4, NZ), bf16),
            jax.ShapeDtypeStruct((HALO * 4, NZ), bf16),
            jax.ShapeDtypeStruct((HALO * 4, NZ), bf16),
        ),
        in_specs=[pl.BlockSpec(memory_space=pltpu.SMEM), vmem],
        out_specs=(vmem, vmem, vmem, vmem),
        scratch_shapes=[pltpu.VMEM((2, ROWS * 4, 128), f32)],
        compiler_params=pltpu.CompilerParams(vmem_limit_bytes=8 << 20),
        name="prepare",
    )(place, image)


def consistency_kernel(
    place_ref, x_ref, kspace_hbm, maps_hbm, other_hbm, sampling_hbm, row_hbm, col_hbm, out_ref,
    mine, other, sampling, row, col, sem
):
    core = place_ref[0]
    copies = [
        pltpu.make_async_copy(source, target, sem.at[i])
        for i, (source, target) in enumerate(
            (
                (maps_hbm.at[core], mine.at[2:4]),
                (col_hbm, col),
                (row_hbm, row),
                (kspace_hbm.at[core], mine.at[0:2]),
                (sampling_hbm, sampling),
                (other_hbm, other),
            )
        )
    ]
    for copy in copies:
        copy.start()

    def dot(left, right):
        return jnp.dot(left, right, preferred_element_type=f32)

    x_real = x_ref[:, 0].astype(f32).reshape(NY, NZ).T
    x_imag = x_ref[:, 1].astype(f32).reshape(NY, NZ).T
    sum_real = jnp.zeros((NZ, NY), f32)
    sum_imag = jnp.zeros((NZ, NY), f32)
    copies[0].wait()
    copies[1].wait()
    for ref in (mine, other):
        if ref is other:
            copies[5].wait()
        map_real = ref[2].astype(f32)
        map_imag = ref[3].astype(f32)
        w_real = (map_real * x_real - map_imag * x_imag).astype(bf16)
        w_imag = (map_real * x_imag + map_imag * x_real).astype(bf16)
        h_real = dot(col[...], jnp.concatenate([w_real, w_imag], 0)).astype(bf16)
        h_imag = dot(col[...], jnp.concatenate([w_imag, -w_real], 0)).astype(bf16)
        if ref is mine:
            for copy in copies[2:5]:
                copy.wait()
        sampled = sampling[...].astype(f32)
        s_real = dot(jnp.concatenate([h_real, h_imag], 1), row[...])
        s_imag = dot(jnp.concatenate([h_imag, -h_real], 1), row[...])
        r_real = (sampled * (s_real - ref[0].astype(f32))).astype(bf16)
        r_imag = (sampled * (s_imag - ref[1].astype(f32))).astype(bf16)
        b_real = dot(jnp.concatenate([r_real, -r_imag], 1), row[...]).astype(bf16)
        b_imag = dot(jnp.concatenate([r_imag, r_real], 1), row[...]).astype(bf16)
        o_real = dot(col[...], jnp.concatenate([b_real, -b_imag], 0))
        o_imag = dot(col[...], jnp.concatenate([b_imag, b_real], 0))
        sum_real = sum_real + map_real * o_real + map_imag * o_imag
        sum_imag = sum_imag + map_real * o_imag - map_imag * o_real
    out_ref[:, 0] = sum_real.T.reshape(COILS, ROWS, NZ).astype(bf16)
    out_ref[:, 1] = sum_imag.T.reshape(COILS, ROWS, NZ).astype(bf16)


def consistency(place, x, kspace, maps, other, sampling, row, col):
    vmem = pl.BlockSpec(memory_space=pltpu.VMEM)
    return pl.pallas_call(
        consistency_kernel,
        out_shape=jax.ShapeDtypeStruct((COILS, 2, ROWS, NZ), bf16),
        in_specs=[pl.BlockSpec(memory_space=pltpu.SMEM), vmem]
        + [pl.BlockSpec(memory_space=pl.ANY)] * 6,
        out_specs=vmem,
        scratch_shapes=[
            pltpu.VMEM((4, NZ, NY), bf16),
            pltpu.VMEM((4, NZ, NY), bf16),
            pltpu.VMEM((NZ, NY), jnp.int32),
            pltpu.VMEM((2 * NY, NY), bf16),
            pltpu.VMEM((NZ, 2 * NZ), bf16),
            pltpu.SemaphoreType.DMA((6,)),
        ],
        compiler_params=pltpu.CompilerParams(vmem_limit_bytes=52 << 20),
        cost_estimate=pl.CostEstimate(
            flops=4_000_000_000, bytes_accessed=3_000_000, transcendentals=0
        ),
        name="consistency",
    )(place, x, kspace, maps, other, sampling, row, col)


def regularizer_kernel(
    place_ref,
    x0_ref,
    x1_ref,
    x2_ref,
    x3_ref,
    taps_ref,
    respond_ref,
    spread_ref,
    thresholds_ref,
    out_ref,
    weights_ref,
    shifted_ref,
    total_ref,
):
    for site in range(3):
        taps = jnp.dot(taps_ref[...], respond_ref[site], preferred_element_type=f32)
        for t in range(BAND):
            rolled = pltpu.roll(taps, 4 * t, 1) if t else taps
            start = (t * 3 + site) * FILTERS
            weights_ref[start : start + FILTERS, :] = rolled.astype(bf16)
    zero = jnp.zeros((2, LINES * 4, 1), f32)
    for e in range(ECHOES):
        ref = (x0_ref, x1_ref, x2_ref, x3_ref)[e // 2]
        x = ref[e % 2].astype(f32)
        shifted_ref[e, 0] = jnp.concatenate([zero, x[:, :, : NZ - 1]], 2).astype(bf16)
        shifted_ref[e, 1] = ref[e % 2]
        shifted_ref[e, 2] = jnp.concatenate([x[:, :, 1:], zero], 2).astype(bf16)
    total_ref[...] = jnp.zeros_like(total_ref)
    spread = spread_ref[...]

    for base, first in zip(BASES, FIRST):
        weights = weights_ref[first * SITES :, : 3 * 2 * WINDOW * 4]
        energy = None
        for e in reversed(range(ECHOES)):
            block = shifted_ref[e, :, :, base * 4 : (base + WINDOW) * 4, :]
            window = block.reshape(3 * 2 * WINDOW * 4, NZ)
            response = jnp.dot(weights, window, preferred_element_type=f32)
            square = response * response
            energy = square if energy is None else energy + square
        magnitude = jnp.sqrt(energy)
        factor = magnitude / (magnitude + thresholds_ref[first * SITES :, :])
        shrunk = response * factor
        if base == 0:
            top = shrunk[:SITES] * place_ref[1].astype(f32)
            shrunk = jnp.concatenate([top, shrunk[SITES:]], 0)
        if base == BASES[-1]:
            bottom = shrunk[-SITES:] * place_ref[2].astype(f32)
            shrunk = jnp.concatenate([shrunk[:-SITES], bottom], 0)
        shrunk = shrunk.astype(bf16)
        for t in range(0, BAND - first, PAIR):
            pair = shrunk[t * SITES : (t + PAIR) * SITES]
            part = jnp.dot(spread, pair, preferred_element_type=f32)
            size = (PAIR + 2) * 4
            start = (base + first + t) * 4
            for d in range(3):
                total_ref[d, start : start + size, :] += part[d * size : (d + 1) * size]
    inner = slice(HALO * 4, (HALO + ROWS) * 4)
    zero = jnp.zeros((ROWS * 4, 1), f32)
    penalty = (
        total_ref[1, inner, :]
        + jnp.concatenate([total_ref[0, inner, 1:], zero], 1)
        + jnp.concatenate([zero, total_ref[2, inner, : NZ - 1]], 1)
    )
    pad = jnp.zeros((ROWS * 4, 256 - NZ), f32)
    out_ref[0] = penalty[:, :128]
    out_ref[1] = jnp.concatenate([penalty[:, 128:], pad], 1)


def regularizer(place, blocks, taps, respond, spread, thresholds):
    vmem = pl.BlockSpec(memory_space=pltpu.VMEM)
    return pl.pallas_call(
        regularizer_kernel,
        out_shape=jax.ShapeDtypeStruct((2, ROWS * 4, 128), f32),
        in_specs=[pl.BlockSpec(memory_space=pltpu.SMEM)] + [vmem] * 8,
        out_specs=vmem,
        scratch_shapes=[
            pltpu.VMEM((BAND * SITES, 256), bf16),
            pltpu.VMEM((ECHOES, 3, 2, LINES * 4, NZ), bf16),
            pltpu.VMEM((3, LINES * 4, NZ), f32),
        ],
        compiler_params=pltpu.CompilerParams(vmem_limit_bytes=20 << 20),
        cost_estimate=pl.CostEstimate(
            flops=9_000_000_000, bytes_accessed=2_000_000, transcendentals=1_000_000
        ),
        name="regularizer",
    )(place, *blocks, taps, respond, spread, thresholds)


def update_kernel(weight_ref, image_ref, arrived_ref, penalty_ref, out_ref):
    for s in range(2):
        for p in range(2):
            total = arrived_ref[s, p].astype(f32)
            for z in range(1, COILS // 2):
                total = total + arrived_ref[2 * z + s, p].astype(f32)
            rows = pl.ds(s * 2 + p, ROWS, stride=4)
            penalty = jnp.concatenate(
                [penalty_ref[0, rows, :], penalty_ref[1, rows, :][:, : NZ - 128]], 1
            )
            out_ref[:, 0, s, p, :] = image_ref[:, 0, s, p, :] - weight_ref[0] * total - penalty


def update(weight, image, arrived, penalty):
    vmem = pl.BlockSpec(memory_space=pltpu.VMEM)
    return pl.pallas_call(
        update_kernel,
        out_shape=jax.ShapeDtypeStruct(image.shape, f32),
        in_specs=[pl.BlockSpec(memory_space=pltpu.SMEM), vmem, vmem, vmem],
        out_specs=vmem,
        compiler_params=pltpu.CompilerParams(vmem_limit_bytes=8 << 20),
        name="update",
    )(weight, image, arrived, penalty)


def body(kspace, sampling, coil_maps, image, filters, thresholds, dc_weight):
    row = jnp.asarray(np.concatenate(np_tables(NY), 0))
    col = jnp.asarray(np.concatenate(np_tables(NZ), 1))
    coil = lax.axis_index("coil")
    core = lax.rem(coil, 2)
    read = lax.axis_index("read")
    place = jnp.stack([core, (coil > 0).astype(jnp.int32), (coil < COILS - 1).astype(jnp.int32)])

    sent, lines, near, far = prepare(place, image)
    gathered = lax.all_to_all(sent, "coil", 0, 0, tiled=True)

    on_chip = [(i, i ^ 1) for i in range(COILS)]
    measured = kspace[:, 0, 0].transpose(1, 2, 3, 0)
    maps = coil_maps[:, 0].transpose(1, 2, 3, 0)
    other = jnp.concatenate(
        [lax.dynamic_index_in_dim(a, 1 - core, 0, keepdims=False) for a in (measured, maps)], 0
    )

    respond, spread = np_expansions()
    taps = filters.reshape(FILTERS, 54)
    respond = lax.dynamic_index_in_dim(jnp.asarray(respond), read, 0, keepdims=False)
    spread = lax.dynamic_index_in_dim(jnp.asarray(spread), read, 0, keepdims=False)
    spread = jnp.einsum("ycl,kc->lyk", spread, taps, preferred_element_type=f32)
    spread = spread.astype(bf16).reshape(48, PAIR * SITES)
    levels = jnp.broadcast_to(jnp.tile(thresholds, BAND * 3)[:, None], (BAND * SITES, NZ))

    near, far, other = lax.optimization_barrier((near, far, other))
    other = lax.ppermute(other, "coil", on_chip)

    even = core == 0
    next_chip = [(i, i + 1) for i in range(1, COILS - 1, 2)]
    next_chip += [(j, i) for i, j in next_chip]
    near = lax.ppermute(near, "coil", on_chip)
    far = lax.ppermute(far, "coil", next_chip)
    above = jnp.where(even, far, near)
    below = jnp.where(even, near, far)
    extended = jnp.concatenate([above, lines, below], 0)

    def swap(block, flip):
        pairs = [(i, i ^ flip) for i in range(2 * ECHOES)]
        return lax.ppermute(block, ("echo", "read"), pairs)

    quad = jnp.stack([extended] + [swap(extended, flip) for flip in (1, 2, 3)])
    quad = quad.reshape(2, 2, LINES * 4, NZ)
    gathered, quad, taps, respond, spread, levels = lax.optimization_barrier(
        (gathered, quad, taps, respond, spread, levels)
    )
    partial = consistency(
        place, gathered, measured, maps, other, sampling[:, 0].T, row, col
    )
    quad, partial = lax.optimization_barrier((quad, partial))
    blocks = [quad] + [swap(quad, flip) for flip in (4, 8, 12)]
    arrived = lax.all_to_all(partial, "coil", 0, 0, tiled=True)
    penalty = regularizer(place, blocks, taps, respond, spread, levels)
    return update(dc_weight, image, arrived, penalty)


def solution(mesh):
    return jax.shard_map(
        body,
        mesh=mesh,
        in_specs=(
            P(None, "echo", "coil", "read", None, None),
            P(None, "echo", None),
            P(None, "coil", "read", None, None),
            P("coil", "echo", "read", None, None),
            P(),
            P(),
            P("echo"),
        ),
        out_specs=P("coil", "echo", "read", None, None),
        check_vma=False,
    )
```

```python
import functools

import jax
import jax.numpy as jnp
import ml_dtypes
import numpy as np
from jax import lax
from jax.experimental import pallas as pl
from jax.experimental.pallas import tpu as pltpu
from jax.sharding import PartitionSpec as P

NY = 384
NZ = 192
FILTERS = 48
ECHOES = 8
COILS = 16
ROWS = NY // COILS
HALO = 2
BAND = 8
WINDOW = BAND + 2
SITES = 3 * FILTERS
PAIR = 2
LINES = ROWS + 2 * HALO
BASES = (0, 8, 16, 18)
FIRST = (0, 0, 0, 6)

bf16 = jnp.bfloat16
f32 = jnp.float32


def np_tables(length):
    positions = np.arange(length, dtype=np.int32)
    product = positions[:, None] * positions[None, :] % length
    phases = product.astype(np.float32) * np.float32(2.0 * np.pi / length)
    normalize = np.float32(length ** (-0.5))
    cos = (np.cos(phases) * normalize).astype(ml_dtypes.bfloat16)
    sin = (np.sin(phases) * normalize).astype(ml_dtypes.bfloat16)
    return cos, sin


def np_expansions():
    respond = np.zeros((2, 3, 54, 256), np.float32)
    spread = np.zeros((2, PAIR * 3, 54, 48), np.float32)
    for read in range(2):
        for site in range(3):
            for a in range(3):
                for b in range(3):
                    for d in range(3):
                        for p in range(2):
                            tap = ((a * 3 + b) * 3 + d) * 2 + p
                            sigma = read + site + b - 1
                            if 0 <= sigma < 4:
                                half = (sigma // 2) ^ read
                                column = ((d * 2 + half) * WINDOW + a) * 4
                                column += (sigma % 2) * 2 + p
                                respond[read, site, tap, column] = 1
                            own = b + site - read - 1
                            if 0 <= own < 2:
                                for t in range(PAIR):
                                    row = (d * (PAIR + 2) + t + a) * 4 + own * 2 + p
                                    spread[read, t * 3 + site, tap, row] = 1
    return respond.astype(ml_dtypes.bfloat16), spread.astype(ml_dtypes.bfloat16)


def prepare_kernel(place_ref, image_ref, sent_ref, lines_ref, near_ref, far_ref, rows_ref):
    pad = jnp.zeros((ROWS, 256 - NZ), f32)
    for s in range(2):
        for p in range(2):
            plane = image_ref[:, 0, s, p, :]
            rows = pl.ds(s * 2 + p, ROWS, stride=4)
            rows_ref[0, rows, :] = plane[:, :128]
            rows_ref[1, rows, :] = jnp.concatenate([plane[:, 128:], pad], 1)
            plane = plane.astype(bf16)
            for z in range(COILS // 2):
                sent_ref[2 * z + s, p] = plane
    lines = jnp.concatenate([rows_ref[0], rows_ref[1, :, : NZ - 128]], 1)
    lines_ref[...] = lines.astype(bf16)
    first = lines[: HALO * 4]
    last = lines[(ROWS - HALO) * 4 :]
    even = place_ref[0] == 0
    near_ref[...] = jnp.where(even, last, first).astype(bf16)
    far_ref[...] = jnp.where(even, first, last).astype(bf16)


def prepare(place, image):
    vmem = pl.BlockSpec(memory_space=pltpu.VMEM)
    return pl.pallas_call(
        prepare_kernel,
        out_shape=(
            jax.ShapeDtypeStruct((COILS, 2, ROWS, NZ), bf16),
            jax.ShapeDtypeStruct((ROWS * 4, NZ), bf16),
            jax.ShapeDtypeStruct((HALO * 4, NZ), bf16),
            jax.ShapeDtypeStruct((HALO * 4, NZ), bf16),
        ),
        in_specs=[pl.BlockSpec(memory_space=pltpu.SMEM), vmem],
        out_specs=(vmem, vmem, vmem, vmem),
        scratch_shapes=[pltpu.VMEM((2, ROWS * 4, 128), f32)],
        compiler_params=pltpu.CompilerParams(vmem_limit_bytes=8 << 20),
        name="prepare",
    )(place, image)


def consistency_kernel(
    place_ref, x_ref, kspace_hbm, maps_hbm, other_k_hbm, other_m_hbm, sampling_hbm, row_hbm, col_hbm, out_ref,
    mine, other, sampling, row, col, sem
):
    core = place_ref[0]
    copies = [
        pltpu.make_async_copy(source, target, sem.at[i])
        for i, (source, target) in enumerate(
            (
                (maps_hbm.at[core], mine.at[2:4]),
                (col_hbm, col),
                (row_hbm, row),
                (kspace_hbm.at[core], mine.at[0:2]),
                (sampling_hbm, sampling),
                (other_m_hbm, other.at[2:4]),
                (other_k_hbm, other.at[0:2]),
            )
        )
    ]
    for copy in copies:
        copy.start()

    def dot(left, right):
        return jnp.dot(left, right, preferred_element_type=f32)

    x_real = x_ref[:, 0].astype(f32).reshape(NY, NZ).T
    x_imag = x_ref[:, 1].astype(f32).reshape(NY, NZ).T
    sum_real = jnp.zeros((NZ, NY), f32)
    sum_imag = jnp.zeros((NZ, NY), f32)
    copies[0].wait()
    copies[1].wait()
    for ref in (mine, other):
        if ref is other:
            copies[5].wait()
            copies[6].wait()
        map_real = ref[2].astype(f32)
        map_imag = ref[3].astype(f32)
        w_real = (map_real * x_real - map_imag * x_imag).astype(bf16)
        w_imag = (map_real * x_imag + map_imag * x_real).astype(bf16)
        h_real = dot(col[...], jnp.concatenate([w_real, w_imag], 0)).astype(bf16)
        h_imag = dot(col[...], jnp.concatenate([w_imag, -w_real], 0)).astype(bf16)
        if ref is mine:
            for copy in copies[2:5]:
                copy.wait()
        sampled = sampling[...].astype(f32)
        s_real = dot(jnp.concatenate([h_real, h_imag], 1), row[...])
        s_imag = dot(jnp.concatenate([h_imag, -h_real], 1), row[...])
        r_real = (sampled * (s_real - ref[0].astype(f32))).astype(bf16)
        r_imag = (sampled * (s_imag - ref[1].astype(f32))).astype(bf16)
        b_real = dot(jnp.concatenate([r_real, -r_imag], 1), row[...]).astype(bf16)
        b_imag = dot(jnp.concatenate([r_imag, r_real], 1), row[...]).astype(bf16)
        o_real = dot(col[...], jnp.concatenate([b_real, -b_imag], 0))
        o_imag = dot(col[...], jnp.concatenate([b_imag, b_real], 0))
        sum_real = sum_real + map_real * o_real + map_imag * o_imag
        sum_imag = sum_imag + map_real * o_imag - map_imag * o_real
    out_ref[:, 0] = sum_real.T.reshape(COILS, ROWS, NZ).astype(bf16)
    out_ref[:, 1] = sum_imag.T.reshape(COILS, ROWS, NZ).astype(bf16)


def consistency(place, x, kspace, maps, other_k, other_m, sampling, row, col):
    vmem = pl.BlockSpec(memory_space=pltpu.VMEM)
    return pl.pallas_call(
        consistency_kernel,
        out_shape=jax.ShapeDtypeStruct((COILS, 2, ROWS, NZ), bf16),
        in_specs=[pl.BlockSpec(memory_space=pltpu.SMEM), vmem]
        + [pl.BlockSpec(memory_space=pl.ANY)] * 7,
        out_specs=vmem,
        scratch_shapes=[
            pltpu.VMEM((4, NZ, NY), bf16),
            pltpu.VMEM((4, NZ, NY), bf16),
            pltpu.VMEM((NZ, NY), jnp.int32),
            pltpu.VMEM((2 * NY, NY), bf16),
            pltpu.VMEM((NZ, 2 * NZ), bf16),
            pltpu.SemaphoreType.DMA((7,)),
        ],
        compiler_params=pltpu.CompilerParams(vmem_limit_bytes=52 << 20),
        cost_estimate=pl.CostEstimate(
            flops=4_000_000_000, bytes_accessed=3_000_000, transcendentals=0
        ),
        name="consistency",
    )(place, x, kspace, maps, other_k, other_m, sampling, row, col)


def regularizer_kernel(
    place_ref,
    x0_ref,
    x1_ref,
    x2_ref,
    x3_ref,
    taps_ref,
    respond_ref,
    spread_ref,
    thresholds_ref,
    out_ref,
    weights_ref,
    shifted_ref,
    total_ref,
):
    for site in range(3):
        taps = jnp.dot(taps_ref[...], respond_ref[site], preferred_element_type=f32)
        for t in range(BAND):
            rolled = pltpu.roll(taps, 4 * t, 1) if t else taps
            start = (t * 3 + site) * FILTERS
            weights_ref[start : start + FILTERS, :] = rolled.astype(bf16)
    zero = jnp.zeros((2, LINES * 4, 1), f32)
    for e in range(ECHOES):
        ref = (x0_ref, x1_ref, x2_ref, x3_ref)[e // 2]
        x = ref[e % 2].astype(f32)
        shifted_ref[e, 0] = jnp.concatenate([zero, x[:, :, : NZ - 1]], 2).astype(bf16)
        shifted_ref[e, 1] = ref[e % 2]
        shifted_ref[e, 2] = jnp.concatenate([x[:, :, 1:], zero], 2).astype(bf16)
    total_ref[...] = jnp.zeros_like(total_ref)
    spread = spread_ref[...]
    levels = jnp.concatenate([thresholds_ref[...]] * (BAND * 3), 0)

    for base, first in zip(BASES, FIRST):
        weights = weights_ref[first * SITES :, : 3 * 2 * WINDOW * 4]
        energy = None
        for e in reversed(range(ECHOES)):
            block = shifted_ref[e, :, :, base * 4 : (base + WINDOW) * 4, :]
            window = block.reshape(3 * 2 * WINDOW * 4, NZ)
            response = jnp.dot(weights, window, preferred_element_type=f32)
            square = response * response
            energy = square if energy is None else energy + square
        magnitude = jnp.sqrt(energy)
        factor = magnitude / (magnitude + levels[first * SITES :, :])
        shrunk = response * factor
        if base == 0:
            top = shrunk[:SITES] * place_ref[1].astype(f32)
            shrunk = jnp.concatenate([top, shrunk[SITES:]], 0)
        if base == BASES[-1]:
            bottom = shrunk[-SITES:] * place_ref[2].astype(f32)
            shrunk = jnp.concatenate([shrunk[:-SITES], bottom], 0)
        shrunk = shrunk.astype(bf16)
        for t in range(0, BAND - first, PAIR):
            pair = shrunk[t * SITES : (t + PAIR) * SITES]
            part = jnp.dot(spread, pair, preferred_element_type=f32)
            size = (PAIR + 2) * 4
            start = (base + first + t) * 4
            for d in range(3):
                total_ref[d, start : start + size, :] += part[d * size : (d + 1) * size]
    inner = slice(HALO * 4, (HALO + ROWS) * 4)
    zero = jnp.zeros((ROWS * 4, 1), f32)
    penalty = (
        total_ref[1, inner, :]
        + jnp.concatenate([total_ref[0, inner, 1:], zero], 1)
        + jnp.concatenate([zero, total_ref[2, inner, : NZ - 1]], 1)
    )
    pad = jnp.zeros((ROWS * 4, 256 - NZ), f32)
    out_ref[0] = penalty[:, :128]
    out_ref[1] = jnp.concatenate([penalty[:, 128:], pad], 1)


def regularizer(place, blocks, taps, respond, spread, thresholds):
    vmem = pl.BlockSpec(memory_space=pltpu.VMEM)
    return pl.pallas_call(
        regularizer_kernel,
        out_shape=jax.ShapeDtypeStruct((2, ROWS * 4, 128), f32),
        in_specs=[pl.BlockSpec(memory_space=pltpu.SMEM)] + [vmem] * 8,
        out_specs=vmem,
        scratch_shapes=[
            pltpu.VMEM((BAND * SITES, 256), bf16),
            pltpu.VMEM((ECHOES, 3, 2, LINES * 4, NZ), bf16),
            pltpu.VMEM((3, LINES * 4, NZ), f32),
        ],
        compiler_params=pltpu.CompilerParams(vmem_limit_bytes=20 << 20),
        cost_estimate=pl.CostEstimate(
            flops=9_000_000_000, bytes_accessed=2_000_000, transcendentals=1_000_000
        ),
        name="regularizer",
    )(place, *blocks, taps, respond, spread, thresholds)


def update_kernel(weight_ref, image_ref, arrived_ref, penalty_ref, out_ref):
    for s in range(2):
        for p in range(2):
            total = arrived_ref[s, p].astype(f32)
            for z in range(1, COILS // 2):
                total = total + arrived_ref[2 * z + s, p].astype(f32)
            rows = pl.ds(s * 2 + p, ROWS, stride=4)
            penalty = jnp.concatenate(
                [penalty_ref[0, rows, :], penalty_ref[1, rows, :][:, : NZ - 128]], 1
            )
            out_ref[:, 0, s, p, :] = image_ref[:, 0, s, p, :] - weight_ref[0] * total - penalty


def update(weight, image, arrived, penalty):
    vmem = pl.BlockSpec(memory_space=pltpu.VMEM)
    return pl.pallas_call(
        update_kernel,
        out_shape=jax.ShapeDtypeStruct(image.shape, f32),
        in_specs=[pl.BlockSpec(memory_space=pltpu.SMEM), vmem, vmem, vmem],
        out_specs=vmem,
        compiler_params=pltpu.CompilerParams(vmem_limit_bytes=8 << 20),
        name="update",
    )(weight, image, arrived, penalty)


def body(kspace, sampling, coil_maps, image, filters, thresholds, dc_weight):
    row = jnp.asarray(np.concatenate(np_tables(NY), 0))
    col = jnp.asarray(np.concatenate(np_tables(NZ), 1))
    coil = lax.axis_index("coil")
    core = lax.rem(coil, 2)
    read = lax.axis_index("read")
    place = jnp.stack([core, (coil > 0).astype(jnp.int32), (coil < COILS - 1).astype(jnp.int32)])

    sent, lines, near, far = prepare(place, image)
    gathered = lax.all_to_all(sent, "coil", 0, 0, tiled=True)

    respond, spread = np_expansions()
    taps = filters.reshape(FILTERS, 54)
    respond = lax.dynamic_index_in_dim(jnp.asarray(respond), read, 0, keepdims=False)
    spread = lax.dynamic_index_in_dim(jnp.asarray(spread), read, 0, keepdims=False)
    spread = jnp.einsum("ycl,kc->lyk", spread, taps, preferred_element_type=f32)
    spread = spread.astype(bf16).reshape(48, PAIR * SITES)
    levels = jnp.broadcast_to(thresholds[:, None], (FILTERS, NZ))

    even = core == 0
    on_chip = [(i, i ^ 1) for i in range(COILS)]
    next_chip = [(i, i + 1) for i in range(1, COILS - 1, 2)]
    next_chip += [(j, i) for i, j in next_chip]
    near = lax.ppermute(near, "coil", on_chip)
    far = lax.ppermute(far, "coil", next_chip)

    measured = kspace[:, 0, 0].transpose(1, 2, 3, 0)
    maps = coil_maps[:, 0].transpose(1, 2, 3, 0)
    own_k, own_m = measured, maps
    above = jnp.where(even, far, near)
    below = jnp.where(even, near, far)
    extended = jnp.concatenate([above, lines, below], 0)
    extended, own_k, own_m = lax.optimization_barrier((extended, own_k, own_m))
    other_k = lax.ppermute(
        lax.dynamic_index_in_dim(own_k, 1 - core, 0, keepdims=False), "coil", on_chip
    )
    other_m = lax.ppermute(
        lax.dynamic_index_in_dim(own_m, 1 - core, 0, keepdims=False), "coil", on_chip
    )

    def swap(block, flip):
        pairs = [(i, i ^ flip) for i in range(2 * ECHOES)]
        return lax.ppermute(block, ("echo", "read"), pairs)

    quad = jnp.stack([extended] + [swap(extended, flip) for flip in (1, 2, 3)])
    quad = quad.reshape(2, 2, LINES * 4, NZ)
    blocks = [quad] + [swap(quad, flip) for flip in (4, 8, 12)]
    gathered, taps, respond, spread, levels = lax.optimization_barrier(
        (gathered, taps, respond, spread, levels)
    )
    partial = consistency(
        place, gathered, measured, maps, other_k, other_m, sampling[:, 0].T, row, col
    )
    arrived = lax.all_to_all(partial, "coil", 0, 0, tiled=True)
    penalty = regularizer(place, blocks, taps, respond, spread, levels)
    return update(dc_weight, image, arrived, penalty)


def solution(mesh):
    return jax.shard_map(
        body,
        mesh=mesh,
        in_specs=(
            P(None, "echo", "coil", "read", None, None),
            P(None, "echo", None),
            P(None, "coil", "read", None, None),
            P("coil", "echo", "read", None, None),
            P(),
            P(),
            P("echo"),
        ),
        out_specs=P("coil", "echo", "read", None, None),
        check_vma=False,
    )
```

```python
import functools

import jax
import jax.numpy as jnp
import ml_dtypes
import numpy as np
from jax import lax
from jax.experimental import pallas as pl
from jax.experimental.pallas import tpu as pltpu
from jax.sharding import PartitionSpec as P

NY = 384
NZ = 192
FILTERS = 48
ECHOES = 8
COILS = 16
ROWS = NY // COILS
HALO = 2
BAND = 8
WINDOW = BAND + 2
SITES = 3 * FILTERS
PAIR = 2
LINES = ROWS + 2 * HALO
BASES = (0, 8, 16, 18)
FIRST = (0, 0, 0, 6)

bf16 = jnp.bfloat16
f32 = jnp.float32


def np_tables(length):
    positions = np.arange(length, dtype=np.int32)
    product = positions[:, None] * positions[None, :] % length
    phases = product.astype(np.float32) * np.float32(2.0 * np.pi / length)
    normalize = np.float32(length ** (-0.5))
    cos = (np.cos(phases) * normalize).astype(ml_dtypes.bfloat16)
    sin = (np.sin(phases) * normalize).astype(ml_dtypes.bfloat16)
    return cos, sin


def np_expansions():
    respond = np.zeros((2, 3, 54, 256), np.float32)
    spread = np.zeros((2, PAIR * 3, 54, 48), np.float32)
    for read in range(2):
        for site in range(3):
            for a in range(3):
                for b in range(3):
                    for d in range(3):
                        for p in range(2):
                            tap = ((a * 3 + b) * 3 + d) * 2 + p
                            sigma = read + site + b - 1
                            if 0 <= sigma < 4:
                                half = (sigma // 2) ^ read
                                column = ((d * 2 + half) * WINDOW + a) * 4
                                column += (sigma % 2) * 2 + p
                                respond[read, site, tap, column] = 1
                            own = b + site - read - 1
                            if 0 <= own < 2:
                                for t in range(PAIR):
                                    row = (d * (PAIR + 2) + t + a) * 4 + own * 2 + p
                                    spread[read, t * 3 + site, tap, row] = 1
    return respond.astype(ml_dtypes.bfloat16), spread.astype(ml_dtypes.bfloat16)


def prepare_kernel(image_ref, sent_ref, lines_ref, near_ref, far_ref, rows_ref):
    pad = jnp.zeros((ROWS, 256 - NZ), f32)
    for s in range(2):
        for p in range(2):
            plane = image_ref[:, 0, s, p, :]
            rows = pl.ds(s * 2 + p, ROWS, stride=4)
            rows_ref[0, rows, :] = plane[:, :128]
            rows_ref[1, rows, :] = jnp.concatenate([plane[:, 128:], pad], 1)
            plane = plane.astype(bf16)
            for z in range(COILS // 2):
                sent_ref[2 * z + s, p] = plane
    lines = jnp.concatenate([rows_ref[0], rows_ref[1, :, : NZ - 128]], 1)
    lines_ref[...] = lines.astype(bf16)
    first = lines[: HALO * 4]
    last = lines[(ROWS - HALO) * 4 :]
    even = lax.rem(lax.axis_index("coil"), 2) == 0
    near_ref[...] = jnp.where(even, last, first).astype(bf16)
    far_ref[...] = jnp.where(even, first, last).astype(bf16)


def prepare(image):
    vmem = pl.BlockSpec(memory_space=pltpu.VMEM)
    return pl.pallas_call(
        prepare_kernel,
        out_shape=(
            jax.ShapeDtypeStruct((COILS, 2, ROWS, NZ), bf16),
            jax.ShapeDtypeStruct((ROWS * 4, NZ), bf16),
            jax.ShapeDtypeStruct((HALO * 4, NZ), bf16),
            jax.ShapeDtypeStruct((HALO * 4, NZ), bf16),
        ),
        in_specs=[vmem],
        out_specs=(vmem, vmem, vmem, vmem),
        scratch_shapes=[pltpu.VMEM((2, ROWS * 4, 128), f32)],
        compiler_params=pltpu.CompilerParams(vmem_limit_bytes=8 << 20),
        name="prepare",
    )(image)


def consistency_kernel(
    x_ref, kspace_hbm, maps_hbm, other_k_hbm, other_m_hbm, sampling_hbm, row_hbm, col_hbm, out_hbm,
    measured, maps, sampling, row, col, out_ref, sem
):
    core = lax.rem(lax.axis_index("coil"), 2)
    copies = [
        pltpu.make_async_copy(source, target, sem.at[i])
        for i, (source, target) in enumerate(
            (
                (maps_hbm.at[core], maps.at[0]),
                (other_m_hbm, maps.at[1]),
                (col_hbm, col),
                (row_hbm, row),
                (kspace_hbm.at[core], measured.at[0]),
                (other_k_hbm, measured.at[1]),
                (sampling_hbm, sampling),
            )
        )
    ]
    for copy in copies:
        copy.start()

    def dot(left, right):
        return jnp.dot(left, right, preferred_element_type=f32)

    x_real = x_ref[:, 0].astype(f32).reshape(NY, NZ).T
    x_imag = x_ref[:, 1].astype(f32).reshape(NY, NZ).T
    for copy in copies[:3]:
        copy.wait()
    columns = []
    for c in range(2):
        map_real = maps[c, 0].astype(f32)
        map_imag = maps[c, 1].astype(f32)
        w_real = (map_real * x_real - map_imag * x_imag).astype(bf16)
        w_imag = (map_real * x_imag + map_imag * x_real).astype(bf16)
        columns.append(jnp.concatenate([w_real, w_imag], 0))
        columns.append(jnp.concatenate([w_imag, -w_real], 0))
    h = dot(col[...], jnp.concatenate(columns, 1)).astype(bf16)
    h = [h[:, i * NY : (i + 1) * NY] for i in range(4)]
    for copy in copies[3:]:
        copy.wait()
    lines = []
    for real, imag in ((h[0], h[1]), (h[2], h[3])):
        lines.append(jnp.concatenate([real, imag], 1))
        lines.append(jnp.concatenate([imag, -real], 1))
    s = dot(jnp.concatenate(lines, 0), row[...])
    sampled = sampling[...].astype(f32)
    r = [
        (sampled * (s[i * NZ : (i + 1) * NZ] - measured[i // 2, i % 2].astype(f32))).astype(bf16)
        for i in range(4)
    ]
    lines = []
    for real, imag in ((r[0], r[1]), (r[2], r[3])):
        lines.append(jnp.concatenate([real, -imag], 1))
        lines.append(jnp.concatenate([imag, real], 1))
    b = dot(jnp.concatenate(lines, 0), row[...]).astype(bf16)
    b = [b[i * NZ : (i + 1) * NZ] for i in range(4)]
    columns = []
    for real, imag in ((b[0], b[1]), (b[2], b[3])):
        columns.append(jnp.concatenate([real, -imag], 0))
        columns.append(jnp.concatenate([imag, real], 0))
    o = dot(col[...], jnp.concatenate(columns, 1))
    o = [o[:, i * NY : (i + 1) * NY] for i in range(4)]
    outs = []
    for part in range(2):
        total = None
        for c in range(2):
            map_real = maps[c, 0].astype(f32)
            map_imag = maps[c, 1].astype(f32)
            if part == 0:
                term = map_real * o[2 * c] + map_imag * o[2 * c + 1]
            else:
                term = map_real * o[2 * c + 1] - map_imag * o[2 * c]
            total = term if total is None else total + term
        out_ref[part] = total.T.reshape(COILS, ROWS, NZ).astype(bf16)
        outs.append(
            pltpu.make_async_copy(out_ref.at[part], out_hbm.at[:, part], sem.at[7 + part])
        )
        outs[-1].start()
    for copy in outs:
        copy.wait()


def consistency(x, kspace, maps, other_k, other_m, sampling, row, col):
    hbm = pl.BlockSpec(memory_space=pl.ANY)
    return pl.pallas_call(
        consistency_kernel,
        out_shape=jax.ShapeDtypeStruct((COILS, 2, ROWS, NZ), bf16),
        in_specs=[pl.BlockSpec(memory_space=pltpu.VMEM)]
        + [hbm] * 7,
        out_specs=hbm,
        scratch_shapes=[
            pltpu.VMEM((2, 2, NZ, NY), bf16),
            pltpu.VMEM((2, 2, NZ, NY), bf16),
            pltpu.VMEM((NZ, NY), jnp.int32),
            pltpu.VMEM((2 * NY, NY), bf16),
            pltpu.VMEM((NZ, 2 * NZ), bf16),
            pltpu.VMEM((2, COILS, ROWS, NZ), bf16),
            pltpu.SemaphoreType.DMA((9,)),
        ],
        compiler_params=pltpu.CompilerParams(vmem_limit_bytes=52 << 20),
        cost_estimate=pl.CostEstimate(
            flops=4_000_000_000, bytes_accessed=3_000_000, transcendentals=0
        ),
        name="consistency",
    )(x, kspace, maps, other_k, other_m, sampling, row, col)


def regularizer_kernel(
    x0_ref,
    x1_ref,
    x2_ref,
    x3_ref,
    taps_ref,
    respond_ref,
    spread_ref,
    thresholds_ref,
    out_ref,
    weights_ref,
    shifted_ref,
    total_ref,
):
    coil = lax.axis_index("coil")
    for site in range(3):
        taps = jnp.dot(taps_ref[...], respond_ref[site], preferred_element_type=f32)
        for t in range(BAND):
            rolled = pltpu.roll(taps, 4 * t, 1) if t else taps
            start = (t * 3 + site) * FILTERS
            weights_ref[start : start + FILTERS, :] = rolled.astype(bf16)
    zero = jnp.zeros((2, LINES * 4, 1), f32)
    for e in range(ECHOES):
        ref = (x0_ref, x1_ref, x2_ref, x3_ref)[e // 2]
        x = ref[e % 2].astype(f32)
        shifted_ref[e, 0] = jnp.concatenate([zero, x[:, :, : NZ - 1]], 2).astype(bf16)
        shifted_ref[e, 1] = ref[e % 2]
        shifted_ref[e, 2] = jnp.concatenate([x[:, :, 1:], zero], 2).astype(bf16)
    total_ref[...] = jnp.zeros_like(total_ref)
    spread = spread_ref[...]
    levels = jnp.concatenate([thresholds_ref[...]] * (BAND * 3), 0)

    for base, first in zip(BASES, FIRST):
        weights = weights_ref[first * SITES :, : 3 * 2 * WINDOW * 4]
        energy = None
        for e in reversed(range(ECHOES)):
            block = shifted_ref[e, :, :, base * 4 : (base + WINDOW) * 4, :]
            window = block.reshape(3 * 2 * WINDOW * 4, NZ)
            response = jnp.dot(weights, window, preferred_element_type=f32)
            square = response * response
            energy = square if energy is None else energy + square
        magnitude = jnp.sqrt(energy)
        factor = magnitude / (magnitude + levels[first * SITES :, :])
        shrunk = response * factor
        if base == 0:
            top = shrunk[:SITES] * (coil > 0).astype(f32)
            shrunk = jnp.concatenate([top, shrunk[SITES:]], 0)
        if base == BASES[-1]:
            bottom = shrunk[-SITES:] * (coil < COILS - 1).astype(f32)
            shrunk = jnp.concatenate([shrunk[:-SITES], bottom], 0)
        shrunk = shrunk.astype(bf16)
        for t in range(0, BAND - first, PAIR):
            pair = shrunk[t * SITES : (t + PAIR) * SITES]
            part = jnp.dot(spread, pair, preferred_element_type=f32)
            size = (PAIR + 2) * 4
            start = (base + first + t) * 4
            for d in range(3):
                total_ref[d, start : start + size, :] += part[d * size : (d + 1) * size]
    inner = slice(HALO * 4, (HALO + ROWS) * 4)
    zero = jnp.zeros((ROWS * 4, 1), f32)
    penalty = (
        total_ref[1, inner, :]
        + jnp.concatenate([total_ref[0, inner, 1:], zero], 1)
        + jnp.concatenate([zero, total_ref[2, inner, : NZ - 1]], 1)
    )
    pad = jnp.zeros((ROWS * 4, 256 - NZ), f32)
    out_ref[0] = penalty[:, :128]
    out_ref[1] = jnp.concatenate([penalty[:, 128:], pad], 1)


def regularizer(blocks, taps, respond, spread, thresholds):
    vmem = pl.BlockSpec(memory_space=pltpu.VMEM)
    return pl.pallas_call(
        regularizer_kernel,
        out_shape=jax.ShapeDtypeStruct((2, ROWS * 4, 128), f32),
        in_specs=[vmem] * 8,
        out_specs=vmem,
        scratch_shapes=[
            pltpu.VMEM((BAND * SITES, 256), bf16),
            pltpu.VMEM((ECHOES, 3, 2, LINES * 4, NZ), bf16),
            pltpu.VMEM((3, LINES * 4, NZ), f32),
        ],
        compiler_params=pltpu.CompilerParams(vmem_limit_bytes=20 << 20),
        cost_estimate=pl.CostEstimate(
            flops=9_000_000_000, bytes_accessed=2_000_000, transcendentals=1_000_000
        ),
        name="regularizer",
    )(*blocks, taps, respond, spread, thresholds)


def update_kernel(weight_ref, image_ref, arrived_ref, penalty_ref, out_ref):
    for s in range(2):
        for p in range(2):
            total = arrived_ref[s, p].astype(f32)
            for z in range(1, COILS // 2):
                total = total + arrived_ref[2 * z + s, p].astype(f32)
            rows = pl.ds(s * 2 + p, ROWS, stride=4)
            penalty = jnp.concatenate(
                [penalty_ref[0, rows, :], penalty_ref[1, rows, :][:, : NZ - 128]], 1
            )
            out_ref[:, 0, s, p, :] = image_ref[:, 0, s, p, :] - weight_ref[0] * total - penalty


def update(weight, image, arrived, penalty):
    vmem = pl.BlockSpec(memory_space=pltpu.VMEM)
    return pl.pallas_call(
        update_kernel,
        out_shape=jax.ShapeDtypeStruct(image.shape, f32),
        in_specs=[pl.BlockSpec(memory_space=pltpu.SMEM), vmem, vmem, vmem],
        out_specs=vmem,
        compiler_params=pltpu.CompilerParams(vmem_limit_bytes=8 << 20),
        name="update",
    )(weight, image, arrived, penalty)


def body(kspace, sampling, coil_maps, image, filters, thresholds, dc_weight):
    row = jnp.asarray(np.concatenate(np_tables(NY), 0))
    col = jnp.asarray(np.concatenate(np_tables(NZ), 1))
    coil = lax.axis_index("coil")
    core = lax.rem(coil, 2)
    read = lax.axis_index("read")

    sent, lines, near, far = prepare(image)
    gathered = lax.all_to_all(sent, "coil", 0, 0, tiled=True)

    respond, spread = np_expansions()
    taps = filters.reshape(FILTERS, 54)
    respond = lax.dynamic_index_in_dim(jnp.asarray(respond), read, 0, keepdims=False)
    spread = lax.dynamic_index_in_dim(jnp.asarray(spread), read, 0, keepdims=False)
    spread = jnp.einsum("ycl,kc->lyk", spread, taps, preferred_element_type=f32)
    spread = spread.astype(bf16).reshape(48, PAIR * SITES)
    levels = jnp.broadcast_to(thresholds[:, None], (FILTERS, NZ))

    even = core == 0
    on_chip = [(i, i ^ 1) for i in range(COILS)]
    next_chip = [(i, i + 1) for i in range(1, COILS - 1, 2)]
    next_chip += [(j, i) for i, j in next_chip]
    near = lax.ppermute(near, "coil", on_chip)
    far = lax.ppermute(far, "coil", next_chip)

    measured = kspace[:, 0, 0].transpose(1, 2, 3, 0)
    maps = coil_maps[:, 0].transpose(1, 2, 3, 0)
    own_k, own_m = measured, maps
    above = jnp.where(even, far, near)
    below = jnp.where(even, near, far)
    extended = jnp.concatenate([above, lines, below], 0)
    extended, own_k, own_m = lax.optimization_barrier((extended, own_k, own_m))
    other_k = lax.ppermute(
        lax.dynamic_index_in_dim(own_k, 1 - core, 0, keepdims=False), "coil", on_chip
    )
    other_m = lax.ppermute(
        lax.dynamic_index_in_dim(own_m, 1 - core, 0, keepdims=False), "coil", on_chip
    )

    def swap(block, flip):
        pairs = [(i, i ^ flip) for i in range(2 * ECHOES)]
        return lax.ppermute(block, ("echo", "read"), pairs)

    quad = jnp.stack([extended] + [swap(extended, flip) for flip in (1, 2, 3)])
    quad = quad.reshape(2, 2, LINES * 4, NZ)
    blocks = [quad] + [swap(quad, flip) for flip in (4, 8, 12)]
    gathered, taps, respond, spread, levels = lax.optimization_barrier(
        (gathered, taps, respond, spread, levels)
    )
    partial = consistency(
        gathered, measured, maps, other_k, other_m, sampling[:, 0].T, row, col
    )
    arrived = lax.all_to_all(partial, "coil", 0, 0, tiled=True)
    penalty = regularizer(blocks, taps, respond, spread, levels)
    return update(dc_weight, image, arrived, penalty)


def solution(mesh):
    return jax.shard_map(
        body,
        mesh=mesh,
        in_specs=(
            P(None, "echo", "coil", "read", None, None),
            P(None, "echo", None),
            P(None, "coil", "read", None, None),
            P("coil", "echo", "read", None, None),
            P(),
            P(),
            P("echo"),
        ),
        out_specs=P("coil", "echo", "read", None, None),
        check_vma=False,
    )
```

```python
import functools

import jax
import jax.numpy as jnp
import ml_dtypes
import numpy as np
from jax import lax
from jax.experimental import pallas as pl
from jax.experimental.pallas import tpu as pltpu
from jax.sharding import PartitionSpec as P

NY = 384
NZ = 192
FILTERS = 48
ECHOES = 8
COILS = 16
ROWS = NY // COILS
HALO = 2
BAND = 8
WINDOW = BAND + 2
SITES = 3 * FILTERS
PAIR = 2
LINES = ROWS + 2 * HALO
BASES = (0, 8, 16, 18)
FIRST = (0, 0, 0, 6)
BACKWARD = list(range(COILS))[::-1]

bf16 = jnp.bfloat16
f32 = jnp.float32


def np_tables(length):
    positions = np.arange(length, dtype=np.int32)
    product = positions[:, None] * positions[None, :] % length
    phases = product.astype(np.float32) * np.float32(2.0 * np.pi / length)
    normalize = np.float32(length ** (-0.5))
    cos = (np.cos(phases) * normalize).astype(ml_dtypes.bfloat16)
    sin = (np.sin(phases) * normalize).astype(ml_dtypes.bfloat16)
    return cos, sin


def np_expansions():
    respond = np.zeros((2, 3, 54, 256), np.float32)
    spread = np.zeros((2, PAIR * 3, 54, 48), np.float32)
    for read in range(2):
        for site in range(3):
            for a in range(3):
                for b in range(3):
                    for d in range(3):
                        for p in range(2):
                            tap = ((a * 3 + b) * 3 + d) * 2 + p
                            sigma = read + site + b - 1
                            if 0 <= sigma < 4:
                                half = (sigma // 2) ^ read
                                column = ((d * 2 + half) * WINDOW + a) * 4
                                column += (sigma % 2) * 2 + p
                                respond[read, site, tap, column] = 1
                            own = b + site - read - 1
                            if 0 <= own < 2:
                                for t in range(PAIR):
                                    row = (d * (PAIR + 2) + t + a) * 4 + own * 2 + p
                                    spread[read, t * 3 + site, tap, row] = 1
    return respond.astype(ml_dtypes.bfloat16), spread.astype(ml_dtypes.bfloat16)


def prepare_kernel(image_ref, sent_ref, lines_ref, near_ref, far_ref, rows_ref):
    pad = jnp.zeros((ROWS, 256 - NZ), f32)
    for s in range(2):
        for p in range(2):
            plane = image_ref[:, 0, s, p, :]
            rows = pl.ds(s * 2 + p, ROWS, stride=4)
            rows_ref[0, rows, :] = plane[:, :128]
            rows_ref[1, rows, :] = jnp.concatenate([plane[:, 128:], pad], 1)
            plane = plane.astype(bf16)
            for z in range(COILS // 2):
                sent_ref[COILS - 1 - 2 * z - s, p] = plane
    lines = jnp.concatenate([rows_ref[0], rows_ref[1, :, : NZ - 128]], 1)
    lines_ref[...] = lines.astype(bf16)
    first = lines[: HALO * 4]
    last = lines[(ROWS - HALO) * 4 :]
    even = lax.rem(lax.axis_index("coil"), 2) == 0
    near_ref[...] = jnp.where(even, last, first).astype(bf16)
    far_ref[...] = jnp.where(even, first, last).astype(bf16)


def prepare(image):
    vmem = pl.BlockSpec(memory_space=pltpu.VMEM)
    return pl.pallas_call(
        prepare_kernel,
        out_shape=(
            jax.ShapeDtypeStruct((COILS, 2, ROWS, NZ), bf16),
            jax.ShapeDtypeStruct((ROWS * 4, NZ), bf16),
            jax.ShapeDtypeStruct((HALO * 4, NZ), bf16),
            jax.ShapeDtypeStruct((HALO * 4, NZ), bf16),
        ),
        in_specs=[vmem],
        out_specs=(vmem, vmem, vmem, vmem),
        scratch_shapes=[pltpu.VMEM((2, ROWS * 4, 128), f32)],
        compiler_params=pltpu.CompilerParams(vmem_limit_bytes=8 << 20),
        name="prepare",
    )(image)


def consistency_kernel(
    x_ref, kspace_hbm, maps_hbm, other_k_hbm, other_m_hbm, sampling_hbm, row_hbm, col_hbm, out_hbm,
    measured, maps, sampling, row, col, out_ref, sem
):
    core = lax.rem(lax.axis_index("coil"), 2)
    copies = [
        pltpu.make_async_copy(source, target, sem.at[i])
        for i, (source, target) in enumerate(
            (
                (maps_hbm.at[core], maps.at[0]),
                (other_m_hbm, maps.at[1]),
                (col_hbm, col),
                (row_hbm, row),
                (kspace_hbm.at[core], measured.at[0]),
                (other_k_hbm, measured.at[1]),
                (sampling_hbm, sampling),
            )
        )
    ]
    for copy in copies:
        copy.start()

    def dot(left, right):
        return jnp.dot(left, right, preferred_element_type=f32)

    x_real = jnp.concatenate([x_ref[c, 0].astype(f32) for c in BACKWARD], 0).T
    x_imag = jnp.concatenate([x_ref[c, 1].astype(f32) for c in BACKWARD], 0).T
    for copy in copies[:3]:
        copy.wait()
    columns = []
    for c in range(2):
        map_real = maps[c, 0].astype(f32)
        map_imag = maps[c, 1].astype(f32)
        w_real = (map_real * x_real - map_imag * x_imag).astype(bf16)
        w_imag = (map_real * x_imag + map_imag * x_real).astype(bf16)
        columns.append(jnp.concatenate([w_real, w_imag], 0))
        columns.append(jnp.concatenate([w_imag, -w_real], 0))
    h = dot(col[...], jnp.concatenate(columns, 1)).astype(bf16)
    h = [h[:, i * NY : (i + 1) * NY] for i in range(4)]
    for copy in copies[3:]:
        copy.wait()
    lines = []
    for real, imag in ((h[0], h[1]), (h[2], h[3])):
        lines.append(jnp.concatenate([real, imag], 1))
        lines.append(jnp.concatenate([imag, -real], 1))
    s = dot(jnp.concatenate(lines, 0), row[...])
    sampled = sampling[...].astype(f32)
    r = [
        (sampled * (s[i * NZ : (i + 1) * NZ] - measured[i // 2, i % 2].astype(f32))).astype(bf16)
        for i in range(4)
    ]
    lines = []
    for real, imag in ((r[0], r[1]), (r[2], r[3])):
        lines.append(jnp.concatenate([real, -imag], 1))
        lines.append(jnp.concatenate([imag, real], 1))
    b = dot(jnp.concatenate(lines, 0), row[...]).astype(bf16)
    b = [b[i * NZ : (i + 1) * NZ] for i in range(4)]
    columns = []
    for real, imag in ((b[0], b[1]), (b[2], b[3])):
        columns.append(jnp.concatenate([real, -imag], 0))
        columns.append(jnp.concatenate([imag, real], 0))
    o = dot(col[...], jnp.concatenate(columns, 1))
    o = [o[:, i * NY : (i + 1) * NY] for i in range(4)]
    outs = []
    for part in range(2):
        total = None
        for c in range(2):
            map_real = maps[c, 0].astype(f32)
            map_imag = maps[c, 1].astype(f32)
            if part == 0:
                term = map_real * o[2 * c] + map_imag * o[2 * c + 1]
            else:
                term = map_real * o[2 * c + 1] - map_imag * o[2 * c]
            total = term if total is None else total + term
        total = total.T.astype(bf16)
        for c in range(COILS):
            out_ref[part, COILS - 1 - c] = total[c * ROWS : (c + 1) * ROWS]
        outs.append(
            pltpu.make_async_copy(out_ref.at[part], out_hbm.at[:, part], sem.at[7 + part])
        )
        outs[-1].start()
    for copy in outs:
        copy.wait()


def consistency(x, kspace, maps, other_k, other_m, sampling, row, col):
    hbm = pl.BlockSpec(memory_space=pl.ANY)
    return pl.pallas_call(
        consistency_kernel,
        out_shape=jax.ShapeDtypeStruct((COILS, 2, ROWS, NZ), bf16),
        in_specs=[pl.BlockSpec(memory_space=pltpu.VMEM)]
        + [hbm] * 7,
        out_specs=hbm,
        scratch_shapes=[
            pltpu.VMEM((2, 2, NZ, NY), bf16),
            pltpu.VMEM((2, 2, NZ, NY), bf16),
            pltpu.VMEM((NZ, NY), jnp.int32),
            pltpu.VMEM((2 * NY, NY), bf16),
            pltpu.VMEM((NZ, 2 * NZ), bf16),
            pltpu.VMEM((2, COILS, ROWS, NZ), bf16),
            pltpu.SemaphoreType.DMA((9,)),
        ],
        compiler_params=pltpu.CompilerParams(vmem_limit_bytes=52 << 20),
        cost_estimate=pl.CostEstimate(
            flops=4_000_000_000, bytes_accessed=3_000_000, transcendentals=0
        ),
        name="consistency",
    )(x, kspace, maps, other_k, other_m, sampling, row, col)


def regularizer_kernel(
    x0_ref,
    x1_ref,
    x2_ref,
    x3_ref,
    taps_ref,
    respond_ref,
    spread_ref,
    thresholds_ref,
    out_ref,
    weights_ref,
    shifted_ref,
    total_ref,
):
    coil = lax.axis_index("coil")
    for site in range(3):
        taps = jnp.dot(taps_ref[...], respond_ref[site], preferred_element_type=f32)
        for t in range(BAND):
            rolled = pltpu.roll(taps, 4 * t, 1) if t else taps
            start = (t * 3 + site) * FILTERS
            weights_ref[start : start + FILTERS, :] = rolled.astype(bf16)
    zero = jnp.zeros((2, LINES * 4, 1), f32)
    for e in range(ECHOES):
        ref = (x0_ref, x1_ref, x2_ref, x3_ref)[e // 2]
        x = ref[e % 2].astype(f32)
        shifted_ref[e, 0] = jnp.concatenate([zero, x[:, :, : NZ - 1]], 2).astype(bf16)
        shifted_ref[e, 1] = ref[e % 2]
        shifted_ref[e, 2] = jnp.concatenate([x[:, :, 1:], zero], 2).astype(bf16)
    total_ref[...] = jnp.zeros_like(total_ref)
    spread = spread_ref[...]
    levels = jnp.concatenate([thresholds_ref[...]] * (BAND * 3), 0)

    for base, first in zip(BASES, FIRST):
        weights = weights_ref[first * SITES :, : 3 * 2 * WINDOW * 4]
        energy = None
        for e in reversed(range(ECHOES)):
            block = shifted_ref[e, :, :, base * 4 : (base + WINDOW) * 4, :]
            window = block.reshape(3 * 2 * WINDOW * 4, NZ)
            response = jnp.dot(weights, window, preferred_element_type=f32)
            square = response * response
            energy = square if energy is None else energy + square
        magnitude = jnp.sqrt(energy)
        factor = magnitude / (magnitude + levels[first * SITES :, :])
        shrunk = response * factor
        if base == 0:
            top = shrunk[:SITES] * (coil > 0).astype(f32)
            shrunk = jnp.concatenate([top, shrunk[SITES:]], 0)
        if base == BASES[-1]:
            bottom = shrunk[-SITES:] * (coil < COILS - 1).astype(f32)
            shrunk = jnp.concatenate([shrunk[:-SITES], bottom], 0)
        shrunk = shrunk.astype(bf16)
        for t in range(0, BAND - first, PAIR):
            pair = shrunk[t * SITES : (t + PAIR) * SITES]
            part = jnp.dot(spread, pair, preferred_element_type=f32)
            size = (PAIR + 2) * 4
            start = (base + first + t) * 4
            for d in range(3):
                total_ref[d, start : start + size, :] += part[d * size : (d + 1) * size]
    inner = slice(HALO * 4, (HALO + ROWS) * 4)
    zero = jnp.zeros((ROWS * 4, 1), f32)
    penalty = (
        total_ref[1, inner, :]
        + jnp.concatenate([total_ref[0, inner, 1:], zero], 1)
        + jnp.concatenate([zero, total_ref[2, inner, : NZ - 1]], 1)
    )
    pad = jnp.zeros((ROWS * 4, 256 - NZ), f32)
    out_ref[0] = penalty[:, :128]
    out_ref[1] = jnp.concatenate([penalty[:, 128:], pad], 1)


def regularizer(blocks, taps, respond, spread, thresholds):
    vmem = pl.BlockSpec(memory_space=pltpu.VMEM)
    return pl.pallas_call(
        regularizer_kernel,
        out_shape=jax.ShapeDtypeStruct((2, ROWS * 4, 128), f32),
        in_specs=[vmem] * 8,
        out_specs=vmem,
        scratch_shapes=[
            pltpu.VMEM((BAND * SITES, 256), bf16),
            pltpu.VMEM((ECHOES, 3, 2, LINES * 4, NZ), bf16),
            pltpu.VMEM((3, LINES * 4, NZ), f32),
        ],
        compiler_params=pltpu.CompilerParams(vmem_limit_bytes=20 << 20),
        cost_estimate=pl.CostEstimate(
            flops=9_000_000_000, bytes_accessed=2_000_000, transcendentals=1_000_000
        ),
        name="regularizer",
    )(*blocks, taps, respond, spread, thresholds)


def update_kernel(weight_ref, image_ref, arrived_ref, penalty_ref, out_ref):
    for s in range(2):
        for p in range(2):
            total = arrived_ref[1 - s, p].astype(f32)
            for z in range(1, COILS // 2):
                total = total + arrived_ref[2 * z + 1 - s, p].astype(f32)
            rows = pl.ds(s * 2 + p, ROWS, stride=4)
            penalty = jnp.concatenate(
                [penalty_ref[0, rows, :], penalty_ref[1, rows, :][:, : NZ - 128]], 1
            )
            out_ref[:, 0, s, p, :] = image_ref[:, 0, s, p, :] - weight_ref[0] * total - penalty


def update(weight, image, arrived, penalty):
    vmem = pl.BlockSpec(memory_space=pltpu.VMEM)
    return pl.pallas_call(
        update_kernel,
        out_shape=jax.ShapeDtypeStruct(image.shape, f32),
        in_specs=[pl.BlockSpec(memory_space=pltpu.SMEM), vmem, vmem, vmem],
        out_specs=vmem,
        compiler_params=pltpu.CompilerParams(vmem_limit_bytes=8 << 20),
        name="update",
    )(weight, image, arrived, penalty)


def body(kspace, sampling, coil_maps, image, filters, thresholds, dc_weight):
    row = jnp.asarray(np.concatenate(np_tables(NY), 0))
    col = jnp.asarray(np.concatenate(np_tables(NZ), 1))
    coil = lax.axis_index("coil")
    core = lax.rem(coil, 2)
    read = lax.axis_index("read")

    sent, lines, near, far = prepare(image)
    gathered = lax.all_to_all(
        sent, "coil", 0, 0, tiled=True, axis_index_groups=[BACKWARD]
    )

    respond, spread = np_expansions()
    taps = filters.reshape(FILTERS, 54)
    respond = lax.dynamic_index_in_dim(jnp.asarray(respond), read, 0, keepdims=False)
    spread = lax.dynamic_index_in_dim(jnp.asarray(spread), read, 0, keepdims=False)
    spread = jnp.einsum("ycl,kc->lyk", spread, taps, preferred_element_type=f32)
    spread = spread.astype(bf16).reshape(48, PAIR * SITES)
    levels = jnp.broadcast_to(thresholds[:, None], (FILTERS, NZ))

    even = core == 0
    on_chip = [(i, i ^ 1) for i in range(COILS)]
    next_chip = [(i, i + 1) for i in range(1, COILS - 1, 2)]
    next_chip += [(j, i) for i, j in next_chip]
    near = lax.ppermute(near, "coil", on_chip)
    far = lax.ppermute(far, "coil", next_chip)

    measured = kspace[:, 0, 0].transpose(1, 2, 3, 0)
    maps = coil_maps[:, 0].transpose(1, 2, 3, 0)
    own_k, own_m = measured, maps
    above = jnp.where(even, far, near)
    below = jnp.where(even, near, far)
    extended = jnp.concatenate([above, lines, below], 0)
    extended, own_k, own_m = lax.optimization_barrier((extended, own_k, own_m))
    other_k = lax.ppermute(
        lax.dynamic_index_in_dim(own_k, 1 - core, 0, keepdims=False), "coil", on_chip
    )
    other_m = lax.ppermute(
        lax.dynamic_index_in_dim(own_m, 1 - core, 0, keepdims=False), "coil", on_chip
    )

    def swap(block, flip):
        pairs = [(i, i ^ flip) for i in range(2 * ECHOES)]
        return lax.ppermute(block, ("echo", "read"), pairs)

    quad = jnp.stack([extended] + [swap(extended, flip) for flip in (1, 2, 3)])
    quad = quad.reshape(2, 2, LINES * 4, NZ)
    blocks = [quad] + [swap(quad, flip) for flip in (4, 8, 12)]
    gathered, taps, respond, spread, levels = lax.optimization_barrier(
        (gathered, taps, respond, spread, levels)
    )
    partial = consistency(
        gathered, measured, maps, other_k, other_m, sampling[:, 0].T, row, col
    )
    arrived = lax.all_to_all(
        partial, "coil", 0, 0, tiled=True, axis_index_groups=[BACKWARD]
    )
    penalty = regularizer(blocks, taps, respond, spread, levels)
    return update(dc_weight, image, arrived, penalty)


def solution(mesh):
    return jax.shard_map(
        body,
        mesh=mesh,
        in_specs=(
            P(None, "echo", "coil", "read", None, None),
            P(None, "echo", None),
            P(None, "coil", "read", None, None),
            P("coil", "echo", "read", None, None),
            P(),
            P(),
            P("echo"),
        ),
        out_specs=P("coil", "echo", "read", None, None),
        check_vma=False,
    )
```

```python
import functools

import jax
import jax.numpy as jnp
import ml_dtypes
import numpy as np
from jax import lax
from jax.experimental import pallas as pl
from jax.experimental.pallas import tpu as pltpu
from jax.sharding import PartitionSpec as P

NY = 384
NZ = 192
FILTERS = 48
ECHOES = 8
COILS = 16
ROWS = NY // COILS
HALO = 2
BAND = 8
WINDOW = BAND + 2
SITES = 3 * FILTERS
PAIR = 2
LINES = ROWS + 2 * HALO
BASES = (0, 8, 16, 18)
FIRST = (0, 0, 0, 6)
BACKWARD = list(range(COILS))[::-1]

bf16 = jnp.bfloat16
f32 = jnp.float32


def np_tables(length):
    positions = np.arange(length, dtype=np.int32)
    product = positions[:, None] * positions[None, :] % length
    phases = product.astype(np.float32) * np.float32(2.0 * np.pi / length)
    normalize = np.float32(length ** (-0.5))
    cos = (np.cos(phases) * normalize).astype(ml_dtypes.bfloat16)
    sin = (np.sin(phases) * normalize).astype(ml_dtypes.bfloat16)
    return cos, sin


def np_expansions():
    respond = np.zeros((2, 3, 54, 256), np.float32)
    spread = np.zeros((2, PAIR * 3, 54, 48), np.float32)
    for read in range(2):
        for site in range(3):
            for a in range(3):
                for b in range(3):
                    for d in range(3):
                        for p in range(2):
                            tap = ((a * 3 + b) * 3 + d) * 2 + p
                            sigma = read + site + b - 1
                            if 0 <= sigma < 4:
                                half = (sigma // 2) ^ read
                                column = ((d * 2 + half) * WINDOW + a) * 4
                                column += (sigma % 2) * 2 + p
                                respond[read, site, tap, column] = 1
                            own = b + site - read - 1
                            if 0 <= own < 2:
                                for t in range(PAIR):
                                    row = (d * (PAIR + 2) + t + a) * 4 + own * 2 + p
                                    spread[read, t * 3 + site, tap, row] = 1
    return respond.astype(ml_dtypes.bfloat16), spread.astype(ml_dtypes.bfloat16)


def prepare_kernel(image_ref, sent_ref, lines_ref, near_ref, far_ref, rows_ref):
    pad = jnp.zeros((ROWS, 256 - NZ), f32)
    for s in range(2):
        for p in range(2):
            plane = image_ref[:, 0, s, p, :]
            rows = pl.ds(s * 2 + p, ROWS, stride=4)
            rows_ref[0, rows, :] = plane[:, :128]
            rows_ref[1, rows, :] = jnp.concatenate([plane[:, 128:], pad], 1)
            plane = plane.astype(bf16)
            for z in range(COILS // 2):
                sent_ref[COILS - 1 - 2 * z - s, p] = plane
    lines = jnp.concatenate([rows_ref[0], rows_ref[1, :, : NZ - 128]], 1)
    lines_ref[...] = lines.astype(bf16)
    first = lines[: HALO * 4]
    last = lines[(ROWS - HALO) * 4 :]
    even = lax.rem(lax.axis_index("coil"), 2) == 0
    near_ref[...] = jnp.where(even, last, first).astype(bf16)
    far_ref[...] = jnp.where(even, first, last).astype(bf16)


def prepare(image):
    vmem = pl.BlockSpec(memory_space=pltpu.VMEM)
    return pl.pallas_call(
        prepare_kernel,
        out_shape=(
            jax.ShapeDtypeStruct((COILS, 2, ROWS, NZ), bf16),
            jax.ShapeDtypeStruct((ROWS * 4, NZ), bf16),
            jax.ShapeDtypeStruct((HALO * 4, NZ), bf16),
            jax.ShapeDtypeStruct((HALO * 4, NZ), bf16),
        ),
        in_specs=[vmem],
        out_specs=(vmem, vmem, vmem, vmem),
        scratch_shapes=[pltpu.VMEM((2, ROWS * 4, 128), f32)],
        compiler_params=pltpu.CompilerParams(vmem_limit_bytes=8 << 20),
        name="prepare",
    )(image)


def consistency_kernel(
    x_ref, kspace_hbm, maps_hbm, other_k_hbm, other_m_hbm, sampling_hbm, row_hbm, col_hbm, out_hbm,
    measured, maps, sampling, row, col, out_ref, sem
):
    core = lax.rem(lax.axis_index("coil"), 2)
    copies = [
        pltpu.make_async_copy(source, target, sem.at[i])
        for i, (source, target) in enumerate(
            (
                (maps_hbm.at[core], maps.at[0]),
                (other_m_hbm, maps.at[1]),
                (col_hbm, col),
                (row_hbm, row),
                (kspace_hbm.at[core], measured.at[0]),
                (other_k_hbm, measured.at[1]),
                (sampling_hbm, sampling),
            )
        )
    ]
    for copy in copies:
        copy.start()

    def dot(left, right):
        return jnp.dot(left, right, preferred_element_type=f32)

    x_real = jnp.concatenate([x_ref[c, 0].astype(f32) for c in BACKWARD], 0).T
    x_imag = jnp.concatenate([x_ref[c, 1].astype(f32) for c in BACKWARD], 0).T
    for copy in copies[:3]:
        copy.wait()
    columns = []
    for c in range(2):
        map_real = maps[c, 0].astype(f32)
        map_imag = maps[c, 1].astype(f32)
        w_real = (map_real * x_real - map_imag * x_imag).astype(bf16)
        w_imag = (map_real * x_imag + map_imag * x_real).astype(bf16)
        columns.append(jnp.concatenate([w_real, w_imag], 0))
        columns.append(jnp.concatenate([w_imag, -w_real], 0))
    h = dot(col[...], jnp.concatenate(columns, 1)).astype(bf16)
    h = [h[:, i * NY : (i + 1) * NY] for i in range(4)]
    for copy in copies[3:]:
        copy.wait()
    lines = []
    for real, imag in ((h[0], h[1]), (h[2], h[3])):
        lines.append(jnp.concatenate([real, imag], 1))
        lines.append(jnp.concatenate([imag, -real], 1))
    s = dot(jnp.concatenate(lines, 0), row[...])
    sampled = sampling[...].astype(f32)
    r = [
        (sampled * (s[i * NZ : (i + 1) * NZ] - measured[i // 2, i % 2].astype(f32))).astype(bf16)
        for i in range(4)
    ]
    lines = []
    for real, imag in ((r[0], r[1]), (r[2], r[3])):
        lines.append(jnp.concatenate([real, -imag], 1))
        lines.append(jnp.concatenate([imag, real], 1))
    b = dot(jnp.concatenate(lines, 0), row[...]).astype(bf16)
    b = [b[i * NZ : (i + 1) * NZ] for i in range(4)]
    columns = []
    for real, imag in ((b[0], b[1]), (b[2], b[3])):
        columns.append(jnp.concatenate([real, -imag], 0))
        columns.append(jnp.concatenate([imag, real], 0))
    o = dot(col[...], jnp.concatenate(columns, 1))
    o = [o[:, i * NY : (i + 1) * NY] for i in range(4)]
    outs = []
    for part in range(2):
        total = None
        for c in range(2):
            map_real = maps[c, 0].astype(f32)
            map_imag = maps[c, 1].astype(f32)
            if part == 0:
                term = map_real * o[2 * c] + map_imag * o[2 * c + 1]
            else:
                term = map_real * o[2 * c + 1] - map_imag * o[2 * c]
            total = term if total is None else total + term
        total = total.astype(bf16).T
        for c in range(COILS):
            out_ref[part, COILS - 1 - c] = total[c * ROWS : (c + 1) * ROWS]
        outs.append(
            pltpu.make_async_copy(out_ref.at[part], out_hbm.at[:, part], sem.at[7 + part])
        )
        outs[-1].start()
    for copy in outs:
        copy.wait()


def consistency(x, kspace, maps, other_k, other_m, sampling, row, col):
    hbm = pl.BlockSpec(memory_space=pl.ANY)
    return pl.pallas_call(
        consistency_kernel,
        out_shape=jax.ShapeDtypeStruct((COILS, 2, ROWS, NZ), bf16),
        in_specs=[pl.BlockSpec(memory_space=pltpu.VMEM)]
        + [hbm] * 7,
        out_specs=hbm,
        scratch_shapes=[
            pltpu.VMEM((2, 2, NZ, NY), bf16),
            pltpu.VMEM((2, 2, NZ, NY), bf16),
            pltpu.VMEM((NZ, NY), jnp.int32),
            pltpu.VMEM((2 * NY, NY), bf16),
            pltpu.VMEM((NZ, 2 * NZ), bf16),
            pltpu.VMEM((2, COILS, ROWS, NZ), bf16),
            pltpu.SemaphoreType.DMA((9,)),
        ],
        compiler_params=pltpu.CompilerParams(vmem_limit_bytes=52 << 20),
        cost_estimate=pl.CostEstimate(
            flops=4_000_000_000, bytes_accessed=3_000_000, transcendentals=0
        ),
        name="consistency",
    )(x, kspace, maps, other_k, other_m, sampling, row, col)


def regularizer_kernel(
    x0_ref,
    x1_ref,
    x2_ref,
    x3_ref,
    taps_ref,
    respond_ref,
    spread_ref,
    thresholds_ref,
    out_ref,
    weights_ref,
    shifted_ref,
    total_ref,
):
    coil = lax.axis_index("coil")
    for site in range(3):
        taps = jnp.dot(taps_ref[...], respond_ref[site], preferred_element_type=f32)
        for t in range(BAND):
            rolled = pltpu.roll(taps, 4 * t, 1) if t else taps
            start = (t * 3 + site) * FILTERS
            weights_ref[start : start + FILTERS, :] = rolled.astype(bf16)
    zero = jnp.zeros((2, LINES * 4, 1), f32)
    for e in range(ECHOES):
        ref = (x0_ref, x1_ref, x2_ref, x3_ref)[e // 2]
        x = ref[e % 2].astype(f32)
        shifted_ref[e, 0] = jnp.concatenate([zero, x[:, :, : NZ - 1]], 2).astype(bf16)
        shifted_ref[e, 1] = ref[e % 2]
        shifted_ref[e, 2] = jnp.concatenate([x[:, :, 1:], zero], 2).astype(bf16)
    total_ref[...] = jnp.zeros_like(total_ref)
    spread = spread_ref[...]
    levels = jnp.concatenate([thresholds_ref[...]] * (BAND * 3), 0)

    for base, first in zip(BASES, FIRST):
        weights = weights_ref[first * SITES :, : 3 * 2 * WINDOW * 4]
        energy = None
        for e in reversed(range(ECHOES)):
            block = shifted_ref[e, :, :, base * 4 : (base + WINDOW) * 4, :]
            window = block.reshape(3 * 2 * WINDOW * 4, NZ)
            response = jnp.dot(weights, window, preferred_element_type=f32)
            square = response * response
            energy = square if energy is None else energy + square
        magnitude = jnp.sqrt(energy)
        factor = magnitude / (magnitude + levels[first * SITES :, :])
        shrunk = response * factor
        if base == 0:
            top = shrunk[:SITES] * (coil > 0).astype(f32)
            shrunk = jnp.concatenate([top, shrunk[SITES:]], 0)
        if base == BASES[-1]:
            bottom = shrunk[-SITES:] * (coil < COILS - 1).astype(f32)
            shrunk = jnp.concatenate([shrunk[:-SITES], bottom], 0)
        shrunk = shrunk.astype(bf16)
        for t in range(0, BAND - first, PAIR):
            pair = shrunk[t * SITES : (t + PAIR) * SITES]
            part = jnp.dot(spread, pair, preferred_element_type=f32)
            size = (PAIR + 2) * 4
            start = (base + first + t) * 4
            for d in range(3):
                total_ref[d, start : start + size, :] += part[d * size : (d + 1) * size]
    inner = slice(HALO * 4, (HALO + ROWS) * 4)
    zero = jnp.zeros((ROWS * 4, 1), f32)
    penalty = (
        total_ref[1, inner, :]
        + jnp.concatenate([total_ref[0, inner, 1:], zero], 1)
        + jnp.concatenate([zero, total_ref[2, inner, : NZ - 1]], 1)
    )
    pad = jnp.zeros((ROWS * 4, 256 - NZ), f32)
    out_ref[0] = penalty[:, :128]
    out_ref[1] = jnp.concatenate([penalty[:, 128:], pad], 1)


def regularizer(blocks, taps, respond, spread, thresholds):
    vmem = pl.BlockSpec(memory_space=pltpu.VMEM)
    return pl.pallas_call(
        regularizer_kernel,
        out_shape=jax.ShapeDtypeStruct((2, ROWS * 4, 128), f32),
        in_specs=[vmem] * 8,
        out_specs=vmem,
        scratch_shapes=[
            pltpu.VMEM((BAND * SITES, 256), bf16),
            pltpu.VMEM((ECHOES, 3, 2, LINES * 4, NZ), bf16),
            pltpu.VMEM((3, LINES * 4, NZ), f32),
        ],
        compiler_params=pltpu.CompilerParams(vmem_limit_bytes=20 << 20),
        cost_estimate=pl.CostEstimate(
            flops=9_000_000_000, bytes_accessed=2_000_000, transcendentals=1_000_000
        ),
        name="regularizer",
    )(*blocks, taps, respond, spread, thresholds)


def update_kernel(weight_ref, image_ref, arrived_ref, penalty_ref, out_ref):
    for s in range(2):
        for p in range(2):
            total = arrived_ref[1 - s, p].astype(f32)
            for z in range(1, COILS // 2):
                total = total + arrived_ref[2 * z + 1 - s, p].astype(f32)
            rows = pl.ds(s * 2 + p, ROWS, stride=4)
            penalty = jnp.concatenate(
                [penalty_ref[0, rows, :], penalty_ref[1, rows, :][:, : NZ - 128]], 1
            )
            out_ref[:, 0, s, p, :] = image_ref[:, 0, s, p, :] - weight_ref[0] * total - penalty


def update(weight, image, arrived, penalty):
    vmem = pl.BlockSpec(memory_space=pltpu.VMEM)
    return pl.pallas_call(
        update_kernel,
        out_shape=jax.ShapeDtypeStruct(image.shape, f32),
        in_specs=[pl.BlockSpec(memory_space=pltpu.SMEM), vmem, vmem, vmem],
        out_specs=vmem,
        compiler_params=pltpu.CompilerParams(vmem_limit_bytes=8 << 20),
        name="update",
    )(weight, image, arrived, penalty)


def body(kspace, sampling, coil_maps, image, filters, thresholds, dc_weight):
    row = jnp.asarray(np.concatenate(np_tables(NY), 0))
    col = jnp.asarray(np.concatenate(np_tables(NZ), 1))
    coil = lax.axis_index("coil")
    core = lax.rem(coil, 2)
    read = lax.axis_index("read")

    sent, lines, near, far = prepare(image)
    gathered = lax.all_to_all(
        sent, "coil", 0, 0, tiled=True, axis_index_groups=[BACKWARD]
    )

    respond, spread = np_expansions()
    taps = filters.reshape(FILTERS, 54)
    respond = lax.dynamic_index_in_dim(jnp.asarray(respond), read, 0, keepdims=False)
    spread = lax.dynamic_index_in_dim(jnp.asarray(spread), read, 0, keepdims=False)
    spread = jnp.einsum("ycl,kc->lyk", spread, taps, preferred_element_type=f32)
    spread = spread.astype(bf16).reshape(48, PAIR * SITES)
    levels = jnp.broadcast_to(thresholds[:, None], (FILTERS, NZ))

    even = core == 0
    on_chip = [(i, i ^ 1) for i in range(COILS)]
    next_chip = [(i, i + 1) for i in range(1, COILS - 1, 2)]
    next_chip += [(j, i) for i, j in next_chip]
    near = lax.ppermute(near, "coil", on_chip)
    far = lax.ppermute(far, "coil", next_chip)

    measured = kspace[:, 0, 0].transpose(1, 2, 3, 0)
    maps = coil_maps[:, 0].transpose(1, 2, 3, 0)
    own_k, own_m = measured, maps
    above = jnp.where(even, far, near)
    below = jnp.where(even, near, far)
    extended = jnp.concatenate([above, lines, below], 0)
    extended, own_k, own_m = lax.optimization_barrier((extended, own_k, own_m))
    other_k = lax.ppermute(
        lax.dynamic_index_in_dim(own_k, 1 - core, 0, keepdims=False), "coil", on_chip
    )
    other_m = lax.ppermute(
        lax.dynamic_index_in_dim(own_m, 1 - core, 0, keepdims=False), "coil", on_chip
    )

    def swap(block, flip):
        pairs = [(i, i ^ flip) for i in range(2 * ECHOES)]
        return lax.ppermute(block, ("echo", "read"), pairs)

    quad = jnp.stack([extended] + [swap(extended, flip) for flip in (1, 2, 3)])
    quad = quad.reshape(2, 2, LINES * 4, NZ)
    blocks = [quad] + [swap(quad, flip) for flip in (4, 8, 12)]
    gathered, taps, respond, spread, levels = lax.optimization_barrier(
        (gathered, taps, respond, spread, levels)
    )
    partial = consistency(
        gathered, measured, maps, other_k, other_m, sampling[:, 0].T, row, col
    )
    arrived = lax.all_to_all(
        partial, "coil", 0, 0, tiled=True, axis_index_groups=[BACKWARD]
    )
    penalty = regularizer(blocks, taps, respond, spread, levels)
    return update(dc_weight, image, arrived, penalty)


def solution(mesh):
    return jax.shard_map(
        body,
        mesh=mesh,
        in_specs=(
            P(None, "echo", "coil", "read", None, None),
            P(None, "echo", None),
            P(None, "coil", "read", None, None),
            P("coil", "echo", "read", None, None),
            P(),
            P(),
            P("echo"),
        ),
        out_specs=P("coil", "echo", "read", None, None),
        check_vma=False,
    )
```
